256 devices in a mesh: seq: 32 (over z, y), head: 8 (over x, core).
Axes of the slice: x: 4, y: 4, z: 8, core: 2. Of those that a mesh axis runs over, the one named last changes fastest.
Arguments:
- queries: bfloat16 [16384, 64, 128], P(('seq', 'head')), may hold values from -6 to 6
- key_heads: bfloat16 [16384, 64, 128], P(('seq', 'head')), may hold values from -6 to 6
- value_heads: bfloat16 [16384, 64, 128], P(('seq', 'head')), may hold values from -6 to 6
- grad_output: bfloat16 [16384, 64, 128], P(('seq', 'head')), may hold values from -6 to 6
- doc_lengths: int32 [16], replicated, may hold values from 1 to 8192, 16384 in all
Outputs:
- query_gradient: bfloat16 [16384, 64, 128], P(('seq', 'head'))
- lookup_derivative: bfloat16 [16384, 64, 128], P(('seq', 'head'))
- content_derivative: bfloat16 [16384, 64, 128], P(('seq', 'head'))
The draws below stay inside these ranges and needn't reach their ends.
Inputs may be any that keep to these rules, and one draw needn't show every extreme that they name: `doc_lengths`: the lengths sum to 16384; the longest is exactly 8192.
All inputs are finite; a program needn't handle non-finite values.
Results may differ from the reference program's by a relative error of at most 0.005.
Values may be sent and summed in bfloat16 or wider, within the bound.
A program may use at most 128 MiB of HBM per device.

```python
import math
import jax
import jax.numpy as jnp
import numpy as np
from jax import lax

H = 64
HD = 128
BLOCK = 256
NDOC = 16
TOKENS = 16384


def steps_of(stream_key, extent, shards, smallest, high):
    gain, own = 1.0, jax.random.fold_in(stream_key, 6)
    for axis_at, blocks in shards:
        heights = jnp.exp(jax.random.uniform(jax.random.fold_in(own, axis_at), (blocks,), jnp.float32, smallest / len(shards), high / len(shards)))
        gain = gain * jnp.repeat(heights, extent[axis_at] // blocks).reshape([-1 if axis == axis_at else 1 for axis in range(len(extent))])
    return gain


def length_profile(amount, total, limit, slope):
    portions = [(1 << 20) // math.isqrt(standing ** slope) + 1 for standing in range(2, amount + 1)]
    surplus, counts = total - limit - (amount - 1), [1] * (amount - 1)
    while surplus > 0:
        candidates = [i for i in range(amount - 1) if counts[i] < limit]
        whole, budget = sum([portions[i] for i in candidates]), surplus
        for i in candidates:
            addition = min(limit - counts[i], max(1, budget * portions[i] // whole), surplus)
            counts[i] = counts[i] + addition
            surplus = surplus - addition
    return np.array([limit] + counts)


def ragged_sizes(own_key, amount, total, bound, skew):
    if amount == 2:
        one = jax.random.randint(own_key, (), max(1, total - bound), min(bound, total - 1) + 1)
        return jnp.stack([one, total - one])
    sizes = jnp.asarray(length_profile(amount, total, bound, skew), jnp.int32)
    pairs = (amount - 1) // 2
    source_of, receiver = sizes[1:1 + 2 * pairs:2], sizes[2:2 + 2 * pairs:2]
    margin = jnp.minimum(source_of - 1, bound - receiver)
    shifted = jax.random.randint(jax.random.fold_in(own_key, 1), (pairs,), 0, 1 << 20) % (margin + 1)
    sizes = sizes.at[1:1 + 2 * pairs:2].set(source_of - shifted).at[2:2 + 2 * pairs:2].set(receiver + shifted)
    return sizes[jax.random.permutation(jax.random.fold_in(own_key, 2), amount)]


def noise(key, extent, width, reach, shards=(), kind=jnp.bfloat16):
    drawn = width * jax.random.normal(key, extent, jnp.float32)
    if shards:
        drawn = drawn * steps_of(key, extent, shards, -0.22, 0.18)
    return jnp.clip(drawn, -reach, reach).astype(kind)


def setup_inputs(seed: int = 0) -> dict:
    splits = jax.random.split(jax.random.key(seed), 6)
    return {
        "queries": noise(splits[0], (TOKENS, H, HD), 1.0, 6.0, ((0, 256),)),
        "key_heads": noise(splits[1], (TOKENS, H, HD), 1.0, 6.0, ((0, 256),)),
        "value_heads": noise(splits[2], (TOKENS, H, HD), 1.0, 6.0, ((0, 256),)),
        "grad_output": noise(splits[3], (TOKENS, H, HD), 1.0, 6.0, ((0, 256),)),
        "doc_lengths": ragged_sizes(splits[4], NDOC, TOKENS, TOKENS // 2, 2).astype(jnp.int32),
    }


def doc_index(doc_lengths, positions):
    ends = jnp.cumsum(doc_lengths).astype(jnp.int32)
    return lax.optimization_barrier(jnp.sum((ends[None, :] <= positions[:, None]).astype(jnp.int32), axis=1)).astype(jnp.int32)

def reference(queries, key_heads, value_heads, grad_output, doc_lengths):
    tokens_all, head_count, head_width = queries.shape
    scaling = 1.0 / math.sqrt(head_width * (tokens_all // 2))
    blocks = tokens_all // BLOCK
    doc_of = doc_index(doc_lengths, jnp.arange(tokens_all, dtype=jnp.int32)).reshape(blocks, BLOCK)

    def split_blocks(array):
        return array.reshape(blocks, BLOCK, head_count, head_width)
    query_blocks = split_blocks(queries)
    key_blocks = split_blocks(key_heads)
    value_blocks = split_blocks(value_heads)
    grad_blocks = split_blocks(grad_output)
    zero_state = jnp.zeros((head_count, head_width, head_width), jnp.float32)
    row_ids = jnp.arange(BLOCK, dtype=jnp.int32)
    causal = row_ids[:, None] >= row_ids[None, :]

    def backward_step(carried, inputs):
        running, next_doc = carried
        query_rows, grad_rows, block_docs = inputs
        state_in = jnp.where(block_docs[-1] == next_doc, running, jnp.float32(0.0))
        first_rows = (block_docs == block_docs[0]).astype(jnp.float32)
        within_block_sum = jnp.einsum('thq,thv->hqv', query_rows.astype(jnp.float32) * first_rows[:, None, None], grad_rows.astype(jnp.float32))
        running = jnp.where(block_docs[0] == next_doc, running, jnp.float32(0.0)) + within_block_sum
        return ((running, block_docs[0]), (scaling * state_in).astype(jnp.bfloat16))
    _, suffix = lax.scan(backward_step, (zero_state, jnp.int32(-1)), (query_blocks, grad_blocks, doc_of), reverse=True)

    def forward_step(carried, inputs):
        running, prev_doc = carried
        query_rows, key_rows, value_rows, grad_rows, block_docs, other_memory = inputs
        state_in = jnp.where(block_docs[0] == prev_doc, running, jnp.float32(0.0))
        first_state = lax.optimization_barrier((scaling * state_in).astype(jnp.bfloat16)).astype(jnp.float32)
        other_memory = lax.optimization_barrier(other_memory).astype(jnp.float32)
        probe_f32 = query_rows.astype(jnp.float32)
        lookup_alone = key_rows.astype(jnp.float32)
        content_alone = value_rows.astype(jnp.float32)
        derivative_alone = grad_rows.astype(jnp.float32)
        same_doc = ((block_docs[:, None] == block_docs[None, :]) & causal).astype(jnp.float32)
        affinity_derivative = jnp.einsum('thd,shd->hts', derivative_alone, content_alone) * scaling * same_doc[None]
        affinity_derivative = lax.optimization_barrier(affinity_derivative.astype(jnp.bfloat16)).astype(jnp.float32)
        affinity_table = jnp.einsum('thd,shd->hts', probe_f32, lookup_alone) * scaling * same_doc[None]
        affinity_table = lax.optimization_barrier(affinity_table.astype(jnp.bfloat16)).astype(jnp.float32)
        leading_head_rows = (block_docs == block_docs[0]).astype(jnp.float32)[:, None, None]
        remaining_lines = (block_docs == block_docs[-1]).astype(jnp.float32)[:, None, None]
        query_gradient = jnp.einsum('lca,alg->clg', affinity_derivative, lookup_alone) + jnp.einsum('dgj,gsj->dgs', derivative_alone * leading_head_rows, first_state)
        lookup_derivative = jnp.einsum('gjh,jgt->hgt', affinity_derivative, probe_f32) + jnp.einsum('lcg,cng->lcn', content_alone * remaining_lines, other_memory)
        content_derivative = jnp.einsum('gjh,jgt->hgt', affinity_table, derivative_alone) + jnp.einsum('qpf,pfe->qpe', lookup_alone * remaining_lines, other_memory)
        final_rows = (block_docs == block_docs[-1]).astype(jnp.float32)
        within_block_sum = jnp.einsum('icy,icf->cyf', lookup_alone * final_rows[:, None, None], content_alone)
        running = jnp.where(block_docs[-1] == prev_doc, running, jnp.float32(0.0)) + within_block_sum
        return ((running, block_docs[-1]), (query_gradient.astype(jnp.bfloat16), lookup_derivative.astype(jnp.bfloat16), content_derivative.astype(jnp.bfloat16)))
    _, (query_gradient, lookup_derivative, content_derivative) = lax.scan(forward_step, (zero_state, jnp.int32(-1)), (query_blocks, key_blocks, value_blocks, grad_blocks, doc_of, suffix))
    shape = (tokens_all, head_count, head_width)
    return (query_gradient.reshape(shape), lookup_derivative.reshape(shape), content_derivative.reshape(shape))
```

```python
import functools
import math

import jax
import jax.numpy as jnp
from jax import lax
from jax.experimental import pallas as pl
from jax.experimental.pallas import tpu as pltpu
from jax.sharding import PartitionSpec as P

MESH = pl.DeviceIdType.MESH
F32 = jnp.float32
BF16 = jnp.bfloat16
NDOC = 16
HD = 128


def dot(a, b, ca, cb):
    return lax.dot_general(a, b, (((ca,), (cb,)), ((), ())), preferred_element_type=F32)


def kernel(
    dims, scaling,
    len_ref, q_ref, k_ref, v_ref, g_ref,
    oq_ref, ok_ref, ov_ref,
    toks, sums, arrived, totals, zgot, ready, entering, part, outs, mask_f, mask_b,
    ends, tab_p, tab_z,
    own_sem, xs_sem, xr_sem, is_sem, ir_sem, zs_sem, zr_sem, os_sem, or_sem, ys_sem, yr_sem, yl_sem,
):
    Z, Y, X, NH, TK = dims
    XY = X * Y
    CHUNKS = NH // XY
    CT = 2 * TK
    PT = XY * CT
    s = lax.axis_index("seq")
    hh = lax.axis_index("head")
    z, y = s // Y, s % Y
    x, c = hh // 2, hh % 2
    other = 1 - c
    me = y * X + x
    ins = (q_ref, k_ref, v_ref, g_ref)
    out_refs = (oq_ref, ok_ref, ov_ref)
    partner = (s, x * 2 + other)

    def at_plane(p):
        return (z * Y + p // X, (p % X) * 2 + c)

    def at_z(t):
        return (t * Y + y, hh)

    def ahead(i):
        return ((y + (i // X + i) % Y) % Y) * X + (x + i % X) % X

    def behind(i):
        return ((y - (i // X + i) % Y + Y) % Y) * X + (x - i % X + X) % X

    def z_step(n):
        return (z + ((n + 1) // 2) * (2 * (n % 2) - 1) + Z) % Z

    barrier = pltpu.get_barrier_semaphore()
    pl.semaphore_signal(barrier, inc=1, device_id=partner, device_id_type=MESH)

    def greet_plane(i, carry):
        pl.semaphore_signal(barrier, inc=1, device_id=at_plane(ahead(i)), device_id_type=MESH)
        return carry

    def greet_z(n, carry):
        pl.semaphore_signal(barrier, inc=1, device_id=at_z(z_step(n)), device_id_type=MESH)
        return carry

    lax.fori_loop(1, XY, greet_plane, 0)
    lax.fori_loop(1, Z, greet_z, 0)

    def own_copy(j, a):
        return pltpu.make_async_copy(
            ins[a].at[pl.ds(c * NH + j * XY, XY)],
            toks.at[a, pl.ds(j * XY, XY), c],
            own_sem.at[j, a],
        )

    def core_copy(j, a):
        return pltpu.make_async_remote_copy(
            src_ref=ins[a].at[pl.ds(other * NH + j * XY, XY)],
            dst_ref=toks.at[a, pl.ds(j * XY, XY), c],
            send_sem=xs_sem.at[j, a],
            recv_sem=xr_sem.at[j, a],
            device_id=partner,
            device_id_type=MESH,
        )

    def core_arrival(j, a):
        return pltpu.make_async_remote_copy(
            src_ref=ins[a].at[pl.ds(other * NH + j * XY, XY)],
            dst_ref=toks.at[a, pl.ds(j * XY, XY), other],
            send_sem=xs_sem.at[j, a],
            recv_sem=xr_sem.at[j, a],
            device_id=partner,
            device_id_type=MESH,
        )

    for j in range(CHUNKS):
        for a in range(4):
            own_copy(j, a).start()
    pl.semaphore_wait(barrier, XY + Z - 1)
    for j in range(CHUNKS):
        for a in range(4):
            core_copy(j, a).start()

    total_len = jnp.int32(0)
    for d in range(NDOC):
        total_len = total_len + len_ref[d]
        ends[d] = total_len

    def same(low, high):
        cut = jnp.int32(0)
        for d in range(NDOC):
            e = ends[d]
            cut = cut + jnp.where((low < e) & (e <= high), 1, 0)
        return jnp.where(cut == 0, 1.0, 0.0).astype(F32)

    def fill_plane(p, carry):
        first = z * PT + p * CT
        last = first + CT - 1
        tab_p[0, p] = same(first - 1, last)
        tab_p[1, p] = same(first - 1, first)
        tab_p[2, p] = same(first, last + 1)
        tab_p[3, p] = same(last, last + 1)
        return carry

    lax.fori_loop(0, XY, fill_plane, 0)

    def fill_z(t, carry):
        tab_z[0, t] = jnp.where(t < z, same((t + 1) * PT - 1, z * PT - 1), 0.0).astype(F32)
        tab_z[1, t] = jnp.where(t > z, same((z + 1) * PT, t * PT), 0.0).astype(F32)
        return carry

    lax.fori_loop(0, Z, fill_z, 0)

    base = (s * X + x) * CT
    rows = base + lax.broadcasted_iota(jnp.int32, (CT, CT), 0)
    cols = base + lax.broadcasted_iota(jnp.int32, (CT, CT), 1)
    row_doc = jnp.zeros((CT, CT), jnp.int32)
    col_doc = jnp.zeros((CT, CT), jnp.int32)
    first_doc = jnp.int32(0)
    last_doc = jnp.int32(0)
    for d in range(NDOC):
        e = ends[d]
        row_doc = row_doc + (e <= rows).astype(jnp.int32)
        col_doc = col_doc + (e <= cols).astype(jnp.int32)
        first_doc = first_doc + jnp.where(e <= base, 1, 0)
        last_doc = last_doc + jnp.where(e <= base + CT - 1, 1, 0)
    in_block = jnp.where((row_doc == col_doc) & (rows >= cols), scaling, 0.0).astype(F32)
    leading = jnp.where(row_doc == first_doc, 1.0, 0.0).astype(F32)
    trailing = jnp.where(row_doc == last_doc, 1.0, 0.0).astype(F32)
    mask_f[0] = in_block
    mask_f[1] = leading
    mask_f[2] = trailing
    mask_b[0] = leading.astype(BF16)
    mask_b[1] = trailing.astype(BF16)

    def tok(a, h):
        return toks[a, h].reshape(CT, HD)

    def send_sum(j, i):
        p = ahead(i)
        return pltpu.make_async_remote_copy(
            src_ref=sums.at[j * XY + p],
            dst_ref=arrived.at[j, me],
            send_sem=is_sem.at[j, i],
            recv_sem=ir_sem.at[j, me],
            device_id=at_plane(p),
            device_id_type=MESH,
        )

    def sum_arrival(j, i):
        p = behind(i)
        return pltpu.make_async_remote_copy(
            src_ref=sums.at[j * XY + p],
            dst_ref=arrived.at[j, p],
            send_sem=is_sem.at[j, i],
            recv_sem=ir_sem.at[j, p],
            device_id=at_plane(p),
            device_id_type=MESH,
        )

    def make_sums(j):
        def step(n, carry):
            i = n % XY
            h = j * XY + ahead(i)
            keys = tok(1, h) * mask_b[1]
            a_sum = (dot(tok(2, h), keys, 0, 0) * scaling).astype(BF16)
            queries = tok(0, h) * mask_b[0]
            b_sum = (dot(tok(3, h), queries, 0, 0) * scaling).astype(BF16)
            sums[h, 0] = a_sum
            sums[h, 1] = b_sum

            @pl.when(i == 0)
            def _():
                arrived[j, me, 0] = a_sum
                arrived[j, me, 1] = b_sum

            @pl.when(n >= 2)
            def _():
                send_sum(j, n - 1).start()

            return carry

        lax.fori_loop(1, XY + 1, step, 0)

    def local_work(j):
        def step(i, carry):
            h = j * XY + i
            q, k, v, g = (tok(a, h) for a in range(4))
            gs = (dot(g, v, 1, 1) * mask_f[0]).astype(BF16)
            sc = (dot(q, k, 1, 1) * mask_f[0]).astype(BF16)
            part[0, h] = dot(gs, k, 1, 0)
            part[1, h] = dot(gs, q, 0, 0)
            part[2, h] = dot(sc, g, 0, 0)
            return carry

        lax.fori_loop(0, XY, step, 0)

    def z_copy(j, n):
        t = z_step(n)
        return pltpu.make_async_remote_copy(
            src_ref=totals.at[j, jnp.where(t < z, 1, 0)],
            dst_ref=zgot.at[j, z],
            send_sem=zs_sem.at[j, n],
            recv_sem=zr_sem.at[j, z],
            device_id=at_z(t),
            device_id_type=MESH,
        )

    def z_arrival(j, t):
        return pltpu.make_async_remote_copy(
            src_ref=totals.at[j, 0],
            dst_ref=zgot.at[j, t],
            send_sem=zs_sem.at[j, 0],
            recv_sem=zr_sem.at[j, t],
            device_id=at_z(t),
            device_id_type=MESH,
        )

    def plane_totals(j):
        def wait_one(i, carry):
            sum_arrival(j, i).wait_recv()
            return carry

        lax.fori_loop(1, XY, wait_one, 0)

        def step(p, carry):
            a, b = carry
            r = XY - 1 - p
            a = tab_p[0, p] * a + arrived[j, p, 0].astype(F32)
            b = tab_p[2, r] * b + arrived[j, r, 1].astype(F32)
            return a, b

        zero = jnp.zeros((HD, HD), F32)
        a, b = lax.fori_loop(0, XY, step, (zero, zero))
        totals[j, 0] = a
        totals[j, 1] = b

    def send_totals(j):
        def step(n, carry):
            z_copy(j, n).start()
            return carry

        lax.fori_loop(1, Z, step, 0)

    def send_entering(j, i):
        p = ahead(i)
        return pltpu.make_async_remote_copy(
            src_ref=ready.at[j, p],
            dst_ref=entering.at[j * XY + me],
            send_sem=os_sem.at[j, i],
            recv_sem=or_sem.at[j, me],
            device_id=at_plane(p),
            device_id_type=MESH,
        )

    def entering_arrival(j, i):
        p = behind(i)
        return pltpu.make_async_remote_copy(
            src_ref=ready.at[j, p],
            dst_ref=entering.at[j * XY + p],
            send_sem=os_sem.at[j, i],
            recv_sem=or_sem.at[j, p],
            device_id=at_plane(p),
            device_id_type=MESH,
        )

    def make_entering(j):
        def add_plane(n, carry):
            a, b = carry
            t = z_step(n)
            z_arrival(j, t).wait_recv()
            got = zgot[j, t]
            return a + tab_z[0, t] * got, b + tab_z[1, t] * got

        zero = jnp.zeros((HD, HD), F32)
        start = lax.fori_loop(1, Z, add_plane, (zero, zero))

        def step(p, carry):
            a, b = carry
            r = XY - 1 - p
            ready[j, p, 0] = (tab_p[1, p] * a).astype(BF16)
            ready[j, r, 1] = (tab_p[3, r] * b).astype(BF16)
            a = tab_p[0, p] * a + arrived[j, p, 0].astype(F32)
            b = tab_p[2, r] * b + arrived[j, r, 1].astype(F32)
            return a, b

        lax.fori_loop(0, XY, step, start)
        entering[j * XY + me] = ready[j, me]

        def send(i, carry):
            send_entering(j, i).start()
            return carry

        lax.fori_loop(1, XY, send, 0)

    def finish(j):
        def step(i, carry):
            p = behind(i)
            h = j * XY + p

            @pl.when(i > 0)
            def _():
                entering_arrival(j, i).wait_recv()

            a = entering[h, 0]
            b = entering[h, 1]
            dq = part[0, h] + mask_f[1] * dot(tok(3, h), a, 1, 0)
            dk = part[1, h] + mask_f[2] * dot(tok(2, h), b, 1, 0)
            dv = part[2, h] + mask_f[2] * dot(tok(1, h), b, 1, 1)
            outs[0, h] = dq.astype(BF16).reshape(2, TK, HD)
            outs[1, h] = dk.astype(BF16).reshape(2, TK, HD)
            outs[2, h] = dv.astype(BF16).reshape(2, TK, HD)
            return carry

        lax.fori_loop(0, XY, step, 0)

    def out_own(j, a):
        return pltpu.make_async_copy(
            outs.at[a, pl.ds(j * XY, XY), c],
            out_refs[a].at[pl.ds(c * NH + j * XY, XY)],
            yl_sem.at[j, a],
        )

    def out_core(j, a):
        return pltpu.make_async_remote_copy(
            src_ref=outs.at[a, pl.ds(j * XY, XY), other],
            dst_ref=out_refs[a].at[pl.ds(c * NH + j * XY, XY)],
            send_sem=ys_sem.at[j, a],
            recv_sem=yr_sem.at[j, a],
            device_id=partner,
            device_id_type=MESH,
        )

    def out_arrival(j, a):
        return pltpu.make_async_remote_copy(
            src_ref=outs.at[a, pl.ds(j * XY, XY), other],
            dst_ref=out_refs[a].at[pl.ds(other * NH + j * XY, XY)],
            send_sem=ys_sem.at[j, a],
            recv_sem=yr_sem.at[j, a],
            device_id=partner,
            device_id_type=MESH,
        )

    for j in range(CHUNKS):
        for a in range(4):
            own_copy(j, a).wait()
            core_arrival(j, a).wait_recv()
        make_sums(j)
    local_work(0)
    for j in range(CHUNKS):
        plane_totals(j)
        if j + 1 < CHUNKS:
            send_totals(j)
            local_work(j + 1)
        else:
            send_totals(j)
    for j in range(CHUNKS):
        make_entering(j)
    for j in range(CHUNKS):
        finish(j)
        for a in range(3):
            out_own(j, a).start()
            out_core(j, a).start()

    for j in range(CHUNKS):
        for a in range(4):
            core_copy(j, a).wait_send()

        def drain(i, carry):
            send_sum(j, i).wait_send()
            send_entering(j, i).wait_send()
            return carry

        lax.fori_loop(1, XY, drain, 0)

        def drain_z(n, carry):
            z_copy(j, n).wait_send()
            return carry

        lax.fori_loop(1, Z, drain_z, 0)
        for a in range(3):
            out_own(j, a).wait()
            out_core(j, a).wait_send()
            out_arrival(j, a).wait_recv()


def exchange(dims, scaling, lengths, q, k, v, g):
    Z, Y, X, NH, TK = dims
    XY = X * Y
    CHUNKS = NH // XY
    CT = 2 * TK
    shape = jax.ShapeDtypeStruct((2 * NH, TK, HD), BF16)
    dma = pltpu.SemaphoreType.DMA
    return pl.pallas_call(
        functools.partial(kernel, dims, scaling),
        out_shape=(shape, shape, shape),
        in_specs=[pl.BlockSpec(memory_space=pltpu.SMEM)] + [pl.BlockSpec(memory_space=pl.ANY)] * 4,
        out_specs=(pl.BlockSpec(memory_space=pl.ANY),) * 3,
        scratch_shapes=[
            pltpu.VMEM((4, NH, 2, TK, HD), BF16),
            pltpu.VMEM((NH, 2, HD, HD), BF16),
            pltpu.VMEM((CHUNKS, XY, 2, HD, HD), BF16),
            pltpu.VMEM((CHUNKS, 2, HD, HD), F32),
            pltpu.VMEM((CHUNKS, Z, HD, HD), F32),
            pltpu.VMEM((CHUNKS, XY, 2, HD, HD), BF16),
            pltpu.VMEM((NH, 2, HD, HD), BF16),
            pltpu.VMEM((3, NH, CT, HD), F32),
            pltpu.VMEM((3, NH, 2, TK, HD), BF16),
            pltpu.VMEM((3, CT, HD), F32),
            pltpu.VMEM((2, CT, HD), BF16),
            pltpu.SMEM((NDOC,), jnp.int32),
            pltpu.SMEM((4, XY), F32),
            pltpu.SMEM((2, Z), F32),
            dma((CHUNKS, 4)),
            dma((CHUNKS, 4)),
            dma((CHUNKS, 4)),
            dma((CHUNKS, XY)),
            dma((CHUNKS, XY)),
            dma((CHUNKS, Z)),
            dma((CHUNKS, Z)),
            dma((CHUNKS, XY)),
            dma((CHUNKS, XY)),
            dma((CHUNKS, 3)),
            dma((CHUNKS, 3)),
            dma((CHUNKS, 3)),
        ],
        compiler_params=pltpu.CompilerParams(
            collective_id=0, has_side_effects=True, vmem_limit_bytes=56 << 20
        ),
    )(lengths, q, k, v, g)


def build(mesh, Z, Y, X):
    def local(queries, key_heads, value_heads, grad_output, doc_lengths):
        tokens, heads, width = queries.shape
        all_tokens = tokens * Z * Y * X * 2
        scaling = 1.0 / math.sqrt(width * (all_tokens // 2))
        dims = (Z, Y, X, heads // 2, tokens)
        by_head = [jnp.swapaxes(t, 0, 1) for t in (queries, key_heads, value_heads, grad_output)]
        results = exchange(dims, scaling, doc_lengths, *by_head)
        return tuple(jnp.swapaxes(t, 0, 1) for t in results)

    placed = P(("seq", "head"), None, None)
    return jax.shard_map(
        local,
        mesh=mesh,
        in_specs=(placed,) * 4 + (P(),),
        out_specs=(placed,) * 3,
        check_vma=False,
    )


def solution(mesh):
    return build(mesh, mesh.shape["seq"] // 4, 4, mesh.shape["head"] // 2)
```

```python
import functools
import math

import jax
import jax.numpy as jnp
from jax import lax
from jax.experimental import pallas as pl
from jax.experimental.pallas import tpu as pltpu
from jax.sharding import PartitionSpec as P

MESH = pl.DeviceIdType.MESH
F32 = jnp.float32
BF16 = jnp.bfloat16
NDOC = 16
HD = 128


def dot(a, b, ca, cb):
    return lax.dot_general(a, b, (((ca,), (cb,)), ((), ())), preferred_element_type=F32)


def kernel(
    dims, scaling,
    len_ref, q_ref, k_ref, v_ref, g_ref,
    oq_ref, ok_ref, ov_ref,
    raw, toks, sums, arrived, totals, zgot, ready, entering, part, outs, swapped, mask_f, mask_b,
    ends, tab_p, tab_z,
    own_sem, xs_sem, xr_sem, is_sem, ir_sem, zs_sem, zr_sem, os_sem, or_sem, ys_sem, yr_sem, yl_sem,
):
    Z, Y, X, NH, TK = dims
    XY = X * Y
    CHUNKS = NH // XY
    PARTS = 2 * CHUNKS
    HALF = HD // 2
    CT = 2 * TK
    PT = XY * CT
    s = lax.axis_index("seq")
    hh = lax.axis_index("head")
    z, y = s // Y, s % Y
    x, c = hh // 2, hh % 2
    other = 1 - c
    me = y * X + x
    ins = (q_ref, k_ref, v_ref, g_ref)
    out_refs = (oq_ref, ok_ref, ov_ref)
    partner = (s, x * 2 + other)

    def at_plane(p):
        return (z * Y + p // X, (p % X) * 2 + c)

    def at_z(t):
        return (t * Y + y, hh)

    def ahead(i):
        return ((y + (i // X + i) % Y) % Y) * X + (x + i % X) % X

    def behind(i):
        return ((y - (i // X + i) % Y + Y) % Y) * X + (x - i % X + X) % X

    def z_step(n):
        return (z + ((n + 1) // 2) * (2 * (n % 2) - 1) + Z) % Z

    barrier = pltpu.get_barrier_semaphore()
    pl.semaphore_signal(barrier, inc=1, device_id=partner, device_id_type=MESH)

    def greet_plane(i, carry):
        pl.semaphore_signal(barrier, inc=1, device_id=at_plane(ahead(i)), device_id_type=MESH)
        return carry

    def greet_z(n, carry):
        pl.semaphore_signal(barrier, inc=1, device_id=at_z(z_step(n)), device_id_type=MESH)
        return carry

    lax.fori_loop(1, XY, greet_plane, 0)
    lax.fori_loop(1, Z, greet_z, 0)

    def own_copy(j, a):
        return pltpu.make_async_copy(
            ins[a].at[:, pl.ds(pl.multiple_of(c * NH + j * XY, 8), XY)],
            raw.at[a, j, c],
            own_sem.at[j, a],
        )

    def core_copy(j, a):
        return pltpu.make_async_remote_copy(
            src_ref=ins[a].at[:, pl.ds(pl.multiple_of(other * NH + j * XY, 8), XY)],
            dst_ref=raw.at[a, j, c],
            send_sem=xs_sem.at[j, a],
            recv_sem=xr_sem.at[j, a],
            device_id=partner,
            device_id_type=MESH,
        )

    def core_arrival(j, a):
        return pltpu.make_async_remote_copy(
            src_ref=ins[a].at[:, pl.ds(pl.multiple_of(other * NH + j * XY, 8), XY)],
            dst_ref=raw.at[a, j, other],
            send_sem=xs_sem.at[j, a],
            recv_sem=xr_sem.at[j, a],
            device_id=partner,
            device_id_type=MESH,
        )

    for j in range(CHUNKS):
        for a in range(4):
            own_copy(j, a).start()
    pl.semaphore_wait(barrier, XY + Z - 1)
    for j in range(CHUNKS):
        for a in range(4):
            core_copy(j, a).start()

    total_len = jnp.int32(0)
    for d in range(NDOC):
        total_len = total_len + len_ref[d]
        ends[d] = total_len

    def same(low, high):
        cut = jnp.int32(0)
        for d in range(NDOC):
            e = ends[d]
            cut = cut + jnp.where((low < e) & (e <= high), 1, 0)
        return jnp.where(cut == 0, 1.0, 0.0).astype(F32)

    def fill_plane(p, carry):
        first = z * PT + p * CT
        last = first + CT - 1
        tab_p[0, p] = same(first - 1, last)
        tab_p[1, p] = same(first - 1, first)
        tab_p[2, p] = same(first, last + 1)
        tab_p[3, p] = same(last, last + 1)
        return carry

    def fill_z(t, carry):
        tab_z[0, t] = jnp.where(t < z, same((t + 1) * PT - 1, z * PT - 1), 0.0).astype(F32)
        tab_z[1, t] = jnp.where(t > z, same((z + 1) * PT, t * PT), 0.0).astype(F32)
        return carry

    base = (s * X + x) * CT
    rows = base + lax.broadcasted_iota(jnp.int32, (CT, CT), 0)
    cols = base + lax.broadcasted_iota(jnp.int32, (CT, CT), 1)
    row_doc = jnp.zeros((CT, CT), jnp.int32)
    col_doc = jnp.zeros((CT, CT), jnp.int32)
    first_doc = jnp.int32(0)
    last_doc = jnp.int32(0)
    for d in range(NDOC):
        e = ends[d]
        row_doc = row_doc + (e <= rows).astype(jnp.int32)
        col_doc = col_doc + (e <= cols).astype(jnp.int32)
        first_doc = first_doc + jnp.where(e <= base, 1, 0)
        last_doc = last_doc + jnp.where(e <= base + CT - 1, 1, 0)
    in_block = jnp.where((row_doc == col_doc) & (rows >= cols), scaling, 0.0).astype(F32)
    leading = jnp.where(row_doc == first_doc, 1.0, 0.0).astype(F32)
    trailing = jnp.where(row_doc == last_doc, 1.0, 0.0).astype(F32)
    mask_f[0] = in_block
    mask_f[1] = leading
    mask_f[2] = trailing
    mask_b[0] = leading.astype(BF16)
    mask_b[1] = trailing.astype(BF16)

    def tok(a, h):
        return toks[a, h].reshape(CT, HD)

    def swap_in(j, core):
        for a in range(4):
            toks[a, pl.ds(j * XY, XY), core] = jnp.swapaxes(raw[a, j, core], 0, 1)

    def send_sum(u, i):
        p = ahead(i)
        return pltpu.make_async_remote_copy(
            src_ref=sums.at[(u // 2) * XY + p, u % 2],
            dst_ref=arrived.at[u, me],
            send_sem=is_sem.at[u, i],
            recv_sem=ir_sem.at[u, me],
            device_id=at_plane(p),
            device_id_type=MESH,
        )

    def sum_arrival(u, i):
        p = behind(i)
        return pltpu.make_async_remote_copy(
            src_ref=sums.at[(u // 2) * XY + p, u % 2],
            dst_ref=arrived.at[u, p],
            send_sem=is_sem.at[u, i],
            recv_sem=ir_sem.at[u, p],
            device_id=at_plane(p),
            device_id_type=MESH,
        )

    def make_sums(j):
        def step(n, carry):
            i = n % XY
            h = j * XY + ahead(i)
            keys = tok(1, h) * mask_b[1]
            a_sum = (dot(tok(2, h), keys, 0, 0) * scaling).astype(BF16).reshape(2, HALF, HD)
            queries = tok(0, h) * mask_b[0]
            b_sum = (dot(tok(3, h), queries, 0, 0) * scaling).astype(BF16).reshape(2, HALF, HD)
            for r in range(2):
                sums[h, r, 0] = a_sum[r]
                sums[h, r, 1] = b_sum[r]

            @pl.when(i == 0)
            def _():
                for r in range(2):
                    arrived[2 * j + r, me, 0] = a_sum[r]
                    arrived[2 * j + r, me, 1] = b_sum[r]

            @pl.when(n >= 2)
            def _():
                send_sum(2 * j, n - 1).start()

            return carry

        lax.fori_loop(1, XY + 1, step, 0)

        def send_rest(i, carry):
            send_sum(2 * j + 1, i).start()
            return carry

        lax.fori_loop(1, XY, send_rest, 0)

    def local_work(low, high):
        def step(h, carry):
            q, k, v, g = (tok(a, h) for a in range(4))
            gs = (dot(g, v, 1, 1) * mask_f[0]).astype(BF16)
            sc = (dot(q, k, 1, 1) * mask_f[0]).astype(BF16)
            part[0, h] = dot(gs, k, 1, 0)
            part[1, h] = dot(gs, q, 0, 0)
            part[2, h] = dot(sc, g, 0, 0)
            return carry

        lax.fori_loop(low, high, step, 0)

    def z_copy(j, n):
        t = z_step(n)
        return pltpu.make_async_remote_copy(
            src_ref=totals.at[j, jnp.where(t < z, 1, 0)],
            dst_ref=zgot.at[j, z],
            send_sem=zs_sem.at[j, n],
            recv_sem=zr_sem.at[j, z],
            device_id=at_z(t),
            device_id_type=MESH,
        )

    def z_arrival(j, t):
        return pltpu.make_async_remote_copy(
            src_ref=totals.at[j, 0],
            dst_ref=zgot.at[j, t],
            send_sem=zs_sem.at[j, 0],
            recv_sem=zr_sem.at[j, t],
            device_id=at_z(t),
            device_id_type=MESH,
        )

    def plane_totals(j):
        def wait_one(i, carry):
            sum_arrival(j, i).wait_recv()
            return carry

        lax.fori_loop(1, XY, wait_one, 0)

        def step(p, carry):
            a, b = carry
            r = XY - 1 - p
            a = tab_p[0, p] * a + arrived[j, p, 0].astype(F32)
            b = tab_p[2, r] * b + arrived[j, r, 1].astype(F32)
            return a, b

        zero = jnp.zeros((HALF, HD), F32)
        a, b = lax.fori_loop(0, XY, step, (zero, zero))
        totals[j, 0] = a
        totals[j, 1] = b

    def send_totals(j):
        def step(n, carry):
            z_copy(j, n).start()
            return carry

        lax.fori_loop(1, Z, step, 0)

    def send_entering(j, i):
        p = ahead(i)
        return pltpu.make_async_remote_copy(
            src_ref=ready.at[j, p],
            dst_ref=entering.at[(j // 2) * XY + me, j % 2],
            send_sem=os_sem.at[j, i],
            recv_sem=or_sem.at[j, me],
            device_id=at_plane(p),
            device_id_type=MESH,
        )

    def entering_arrival(j, i):
        p = behind(i)
        return pltpu.make_async_remote_copy(
            src_ref=ready.at[j, p],
            dst_ref=entering.at[(j // 2) * XY + p, j % 2],
            send_sem=os_sem.at[j, i],
            recv_sem=or_sem.at[j, p],
            device_id=at_plane(p),
            device_id_type=MESH,
        )

    def make_entering(j):
        def add_plane(n, carry):
            a, b = carry
            t = z_step(n)
            z_arrival(j, t).wait_recv()
            got = zgot[j, t]
            return a + tab_z[0, t] * got, b + tab_z[1, t] * got

        zero = jnp.zeros((HALF, HD), F32)
        start = lax.fori_loop(1, Z, add_plane, (zero, zero))

        def step(p, carry):
            a, b = carry
            r = XY - 1 - p
            ready[j, p, 0] = (tab_p[1, p] * a).astype(BF16)
            ready[j, r, 1] = (tab_p[3, r] * b).astype(BF16)
            a = tab_p[0, p] * a + arrived[j, p, 0].astype(F32)
            b = tab_p[2, r] * b + arrived[j, r, 1].astype(F32)
            return a, b

        lax.fori_loop(0, XY, step, start)
        entering[(j // 2) * XY + me, j % 2] = ready[j, me]

        def send(i, carry):
            send_entering(j, i).start()
            return carry

        lax.fori_loop(1, XY, send, 0)

    def finish(j):
        def step(i, carry):
            p = behind(i)
            h = j * XY + p

            @pl.when(i > 0)
            def _():
                entering_arrival(2 * j, i).wait_recv()
                entering_arrival(2 * j + 1, i).wait_recv()

            a = entering[h, :, 0].reshape(HD, HD)
            b = entering[h, :, 1].reshape(HD, HD)
            dq = part[0, h] + mask_f[1] * dot(tok(3, h), a, 1, 0)
            dk = part[1, h] + mask_f[2] * dot(tok(2, h), b, 1, 0)
            dv = part[2, h] + mask_f[2] * dot(tok(1, h), b, 1, 1)
            outs[0, h] = dq.astype(BF16).reshape(2, TK, HD)
            outs[1, h] = dk.astype(BF16).reshape(2, TK, HD)
            outs[2, h] = dv.astype(BF16).reshape(2, TK, HD)
            return carry

        lax.fori_loop(0, XY, step, 0)
        for a in range(3):
            for core in range(2):
                swapped[a, j, core] = jnp.swapaxes(outs[a, pl.ds(j * XY, XY), core], 0, 1)

    def out_own(j, a):
        return pltpu.make_async_copy(
            swapped.at[a, j, c],
            out_refs[a].at[:, pl.ds(pl.multiple_of(c * NH + j * XY, 8), XY)],
            yl_sem.at[j, a],
        )

    def out_core(j, a):
        return pltpu.make_async_remote_copy(
            src_ref=swapped.at[a, j, other],
            dst_ref=out_refs[a].at[:, pl.ds(pl.multiple_of(c * NH + j * XY, 8), XY)],
            send_sem=ys_sem.at[j, a],
            recv_sem=yr_sem.at[j, a],
            device_id=partner,
            device_id_type=MESH,
        )

    def out_arrival(j, a):
        return pltpu.make_async_remote_copy(
            src_ref=swapped.at[a, j, other],
            dst_ref=out_refs[a].at[:, pl.ds(pl.multiple_of(other * NH + j * XY, 8), XY)],
            send_sem=ys_sem.at[j, a],
            recv_sem=yr_sem.at[j, a],
            device_id=partner,
            device_id_type=MESH,
        )

    for j in range(CHUNKS):
        for a in range(4):
            own_copy(j, a).wait()
        swap_in(j, c)
    for j in range(CHUNKS):
        for a in range(4):
            core_arrival(j, a).wait_recv()
        swap_in(j, other)
        make_sums(j)
    lax.fori_loop(0, XY, fill_plane, 0)
    lax.fori_loop(0, Z, fill_z, 0)

    def gather(u):
        plane_totals(u)
        send_totals(u)

    piece = NH // PARTS
    for u in range(PARTS):
        local_work(u * piece, (u + 1) * piece)
        gather(u)
        if u >= 2:
            make_entering(u - 2)
    make_entering(PARTS - 2)
    make_entering(PARTS - 1)
    for j in range(CHUNKS):
        finish(j)
        for a in range(3):
            out_own(j, a).start()
            out_core(j, a).start()

    for u in range(PARTS):

        def drain(i, carry):
            send_sum(u, i).wait_send()
            send_entering(u, i).wait_send()
            return carry

        lax.fori_loop(1, XY, drain, 0)

        def drain_z(n, carry):
            z_copy(u, n).wait_send()
            return carry

        lax.fori_loop(1, Z, drain_z, 0)
    for j in range(CHUNKS):
        for a in range(4):
            core_copy(j, a).wait_send()
        for a in range(3):
            out_own(j, a).wait()
            out_core(j, a).wait_send()
            out_arrival(j, a).wait_recv()


def exchange(dims, scaling, lengths, q, k, v, g):
    Z, Y, X, NH, TK = dims
    XY = X * Y
    CHUNKS = NH // XY
    CT = 2 * TK
    PARTS = 2 * CHUNKS
    HALF = HD // 2
    shape = jax.ShapeDtypeStruct((TK, 2 * NH, HD), BF16)
    dma = pltpu.SemaphoreType.DMA
    return pl.pallas_call(
        functools.partial(kernel, dims, scaling),
        out_shape=(shape, shape, shape),
        in_specs=[pl.BlockSpec(memory_space=pltpu.SMEM)] + [pl.BlockSpec(memory_space=pl.ANY)] * 4,
        out_specs=(pl.BlockSpec(memory_space=pl.ANY),) * 3,
        scratch_shapes=[
            pltpu.VMEM((4, CHUNKS, 2, TK, XY, HD), BF16),
            pltpu.VMEM((4, NH, 2, TK, HD), BF16),
            pltpu.VMEM((NH, 2, 2, HALF, HD), BF16),
            pltpu.VMEM((PARTS, XY, 2, HALF, HD), BF16),
            pltpu.VMEM((PARTS, 2, HALF, HD), F32),
            pltpu.VMEM((PARTS, Z, HALF, HD), F32),
            pltpu.VMEM((PARTS, XY, 2, HALF, HD), BF16),
            pltpu.VMEM((NH, 2, 2, HALF, HD), BF16),
            pltpu.VMEM((3, NH, CT, HD), F32),
            pltpu.VMEM((3, NH, 2, TK, HD), BF16),
            pltpu.VMEM((3, CHUNKS, 2, TK, XY, HD), BF16),
            pltpu.VMEM((3, CT, HD), F32),
            pltpu.VMEM((2, CT, HD), BF16),
            pltpu.SMEM((NDOC,), jnp.int32),
            pltpu.SMEM((4, XY), F32),
            pltpu.SMEM((2, Z), F32),
            dma((CHUNKS, 4)),
            dma((CHUNKS, 4)),
            dma((CHUNKS, 4)),
            dma((PARTS, XY)),
            dma((PARTS, XY)),
            dma((PARTS, Z)),
            dma((PARTS, Z)),
            dma((PARTS, XY)),
            dma((PARTS, XY)),
            dma((CHUNKS, 3)),
            dma((CHUNKS, 3)),
            dma((CHUNKS, 3)),
        ],
        compiler_params=pltpu.CompilerParams(
            collective_id=0, has_side_effects=True, vmem_limit_bytes=56 << 20
        ),
    )(lengths, q, k, v, g)


def build(mesh, Z, Y, X):
    def local(queries, key_heads, value_heads, grad_output, doc_lengths):
        tokens, heads, width = queries.shape
        all_tokens = tokens * Z * Y * X * 2
        scaling = 1.0 / math.sqrt(width * (all_tokens // 2))
        dims = (Z, Y, X, heads // 2, tokens)
        return exchange(dims, scaling, doc_lengths, queries, key_heads, value_heads, grad_output)

    placed = P(("seq", "head"), None, None)
    return jax.shard_map(
        local,
        mesh=mesh,
        in_specs=(placed,) * 4 + (P(),),
        out_specs=(placed,) * 3,
        check_vma=False,
    )


def solution(mesh):
    return build(mesh, mesh.shape["seq"] // 4, 4, mesh.shape["head"] // 2)
```

```python
import functools
import math

import jax
import jax.numpy as jnp
from jax import lax
from jax.experimental import pallas as pl
from jax.experimental.pallas import tpu as pltpu
from jax.sharding import PartitionSpec as P

MESH = pl.DeviceIdType.MESH
F32 = jnp.float32
BF16 = jnp.bfloat16
NDOC = 16
HD = 128


STEPS = (
    (0, 0), (2, 2), (3, 2), (2, 3), (1, 2), (2, 1), (0, 2), (2, 0),
    (3, 1), (1, 3), (3, 3), (1, 1), (0, 3), (3, 0), (0, 1), (1, 0),
)
STEPS_X = sum(dx << (2 * i) for i, (dx, dy) in enumerate(STEPS))
STEPS_Y = sum(dy << (2 * i) for i, (dx, dy) in enumerate(STEPS))


def dot(a, b, ca, cb):
    return lax.dot_general(a, b, (((ca,), (cb,)), ((), ())), preferred_element_type=F32)


def kernel(
    dims, scaling,
    len_ref, q_ref, k_ref, v_ref, g_ref,
    oq_ref, ok_ref, ov_ref,
    raw, toks, sums, arrived, totals, zgot, ready, entering, part, outs, swapped, mask_f, mask_b,
    ends, tab_p, tab_z,
    own_sem, xs_sem, xr_sem, is_sem, ir_sem, zs_sem, zr_sem, os_sem, or_sem, last_sem, ys_sem, yr_sem, yl_sem,
):
    Z, Y, X, NH, TK = dims
    XY = X * Y
    CHUNKS = NH // XY
    PARTS = 2 * CHUNKS
    HALF = HD // 2
    CT = 2 * TK
    PT = XY * CT
    s = lax.axis_index("seq")
    hh = lax.axis_index("head")
    z, y = s // Y, s % Y
    x, c = hh // 2, hh % 2
    other = 1 - c
    me = y * X + x
    ins = (q_ref, k_ref, v_ref, g_ref)
    out_refs = (oq_ref, ok_ref, ov_ref)
    partner = (s, x * 2 + other)

    def at_plane(p):
        return (z * Y + p // X, (p % X) * 2 + c)

    def at_z(t):
        return (t * Y + y, hh)

    def plane_step(dx, dy):
        return (z * Y + (y + dy) % Y, ((x + dx) % X) * 2 + c)

    def offset(i):
        return (STEPS_X >> (2 * i)) & 3, (STEPS_Y >> (2 * i)) & 3

    def ahead(i):
        dx, dy = offset(i)
        return ((y + dy) % Y) * X + (x + dx) % X

    def behind(i):
        dx, dy = offset(i)
        return ((y - dy + Y) % Y) * X + (x - dx + X) % X

    def z_step(n):
        return (z + (((n + 1) // 2) if n % 2 else Z - n // 2)) % Z

    barrier = pltpu.get_barrier_semaphore()

    def greet(device):
        pl.semaphore_signal(barrier, inc=1, device_id=device, device_id_type=MESH)

    for n in range(Z - 1, 3, -1):
        greet(at_z(z_step(n)))
    for dx, dy in STEPS[1:]:
        greet(plane_step(dx, dy))
    for n in range(3, 0, -1):
        greet(at_z(z_step(n)))
    greet(partner)

    def own_copy(j, a):
        return pltpu.make_async_copy(
            ins[a].at[:, pl.ds(pl.multiple_of(c * NH + j * XY, 8), XY)],
            raw.at[a, j, c],
            own_sem.at[j, a],
        )

    def core_copy(j, a):
        return pltpu.make_async_remote_copy(
            src_ref=ins[a].at[:, pl.ds(pl.multiple_of(other * NH + j * XY, 8), XY)],
            dst_ref=raw.at[a, j, c],
            send_sem=xs_sem.at[j, a],
            recv_sem=xr_sem.at[j, a],
            device_id=partner,
            device_id_type=MESH,
        )

    def core_arrival(j, a):
        return pltpu.make_async_remote_copy(
            src_ref=ins[a].at[:, pl.ds(pl.multiple_of(other * NH + j * XY, 8), XY)],
            dst_ref=raw.at[a, j, other],
            send_sem=xs_sem.at[j, a],
            recv_sem=xr_sem.at[j, a],
            device_id=partner,
            device_id_type=MESH,
        )

    for j in range(CHUNKS):
        for a in range(4):
            own_copy(j, a).start()

    total_len = jnp.int32(0)
    for d in range(NDOC):
        total_len = total_len + len_ref[d]
        ends[d] = total_len

    def same(low, high):
        cut = jnp.int32(0)
        for d in range(NDOC):
            e = ends[d]
            cut = cut + jnp.where((low < e) & (e <= high), 1, 0)
        return jnp.where(cut == 0, 1.0, 0.0).astype(F32)

    def fill_plane(p, carry):
        first = z * PT + p * CT
        last = first + CT - 1
        tab_p[0, p] = same(first - 1, last)
        tab_p[1, p] = same(first - 1, first)
        tab_p[2, p] = same(first, last + 1)
        tab_p[3, p] = same(last, last + 1)
        return carry

    def fill_z(t, carry):
        tab_z[0, t] = jnp.where(t < z, same((t + 1) * PT - 1, z * PT - 1), 0.0).astype(F32)
        tab_z[1, t] = jnp.where(t > z, same((z + 1) * PT, t * PT), 0.0).astype(F32)
        return carry

    base = (s * X + x) * CT
    rows = base + lax.broadcasted_iota(jnp.int32, (CT, CT), 0)
    cols = base + lax.broadcasted_iota(jnp.int32, (CT, CT), 1)
    row_doc = jnp.zeros((CT, CT), jnp.int32)
    col_doc = jnp.zeros((CT, CT), jnp.int32)
    first_doc = jnp.int32(0)
    last_doc = jnp.int32(0)
    for d in range(NDOC):
        e = ends[d]
        row_doc = row_doc + (e <= rows).astype(jnp.int32)
        col_doc = col_doc + (e <= cols).astype(jnp.int32)
        first_doc = first_doc + jnp.where(e <= base, 1, 0)
        last_doc = last_doc + jnp.where(e <= base + CT - 1, 1, 0)
    in_block = jnp.where((row_doc == col_doc) & (rows >= cols), scaling, 0.0).astype(F32)
    leading = jnp.where(row_doc == first_doc, 1.0, 0.0).astype(F32)
    trailing = jnp.where(row_doc == last_doc, 1.0, 0.0).astype(F32)
    mask_f[0] = in_block
    mask_f[1] = leading
    mask_f[2] = trailing
    mask_b[0] = leading.astype(BF16)
    mask_b[1] = trailing.astype(BF16)

    def tok(a, h):
        return toks[a, h].reshape(CT, HD)

    def swap_in(j, core):
        for a in range(4):
            toks[a, pl.ds(j * XY, XY), core] = jnp.swapaxes(raw[a, j, core], 0, 1)

    def send_sum(u, i):
        p = ahead(i)
        return pltpu.make_async_remote_copy(
            src_ref=sums.at[(u // 2) * XY + p, u % 2],
            dst_ref=arrived.at[u, me],
            send_sem=is_sem.at[u],
            recv_sem=ir_sem.at[u],
            device_id=at_plane(p),
            device_id_type=MESH,
        )

    def all_sums(u):
        block = arrived.at[u, pl.ds(0, XY - 1)]
        return pltpu.make_async_remote_copy(
            src_ref=block,
            dst_ref=block,
            send_sem=is_sem.at[u],
            recv_sem=ir_sem.at[u],
            device_id=partner,
            device_id_type=MESH,
        )

    def make_sums(j):
        def step(n, carry):
            i = n % XY
            h = j * XY + ahead(i)
            keys = tok(1, h) * mask_b[1]
            a_sum = (dot(tok(2, h), keys, 0, 0) * scaling).astype(BF16).reshape(2, HALF, HD)
            queries = tok(0, h) * mask_b[0]
            b_sum = (dot(tok(3, h), queries, 0, 0) * scaling).astype(BF16).reshape(2, HALF, HD)
            for r in range(2):
                sums[h, r, 0] = a_sum[r]
                sums[h, r, 1] = b_sum[r]

            @pl.when(i == 0)
            def _():
                for r in range(2):
                    arrived[2 * j + r, me, 0] = a_sum[r]
                    arrived[2 * j + r, me, 1] = b_sum[r]

            @pl.when(n >= 2)
            def _():
                send_sum(2 * j, n - 1).start()

            return carry

        lax.fori_loop(1, XY + 1, step, 0)

        for i in range(1, XY):
            send_sum(2 * j + 1, i).start()

    def local_work(low, high):
        def step(h, carry):
            q, k, v, g = (tok(a, h) for a in range(4))
            gs = (dot(g, v, 1, 1) * mask_f[0]).astype(BF16)
            sc = (dot(q, k, 1, 1) * mask_f[0]).astype(BF16)
            part[0, h] = dot(gs, k, 1, 0)
            part[1, h] = dot(gs, q, 0, 0)
            part[2, h] = dot(sc, g, 0, 0)
            return carry

        lax.fori_loop(low, high, step, 0)

    def z_copy(u, n):
        t = z_step(n)
        return pltpu.make_async_remote_copy(
            src_ref=totals.at[u, jnp.where(t < z, 1, 0)],
            dst_ref=zgot.at[u, z],
            send_sem=zs_sem.at[u],
            recv_sem=zr_sem.at[u],
            device_id=at_z(t),
            device_id_type=MESH,
        )

    def all_z(u):
        block = zgot.at[u, pl.ds(0, Z - 1)]
        return pltpu.make_async_remote_copy(
            src_ref=block,
            dst_ref=block,
            send_sem=zs_sem.at[u],
            recv_sem=zr_sem.at[u],
            device_id=partner,
            device_id_type=MESH,
        )

    def plane_totals(j):
        all_sums(j).wait_recv()

        def step(p, carry):
            a, b = carry
            r = XY - 1 - p
            a = tab_p[0, p] * a + arrived[j, p, 0].astype(F32)
            b = tab_p[2, r] * b + arrived[j, r, 1].astype(F32)
            return a, b

        zero = jnp.zeros((HALF, HD), F32)
        a, b = lax.fori_loop(0, XY, step, (zero, zero))
        totals[j, 0] = a
        totals[j, 1] = b

    def send_totals(j):
        for n in range(1, Z):
            z_copy(j, n).start()

    def entering_sem(u, p):
        return last_sem.at[p] if u == PARTS - 1 else or_sem.at[u]

    def send_entering(u, i):
        p = ahead(i)
        return pltpu.make_async_remote_copy(
            src_ref=ready.at[u, p],
            dst_ref=entering.at[(u // 2) * XY + me, u % 2],
            send_sem=os_sem.at[u],
            recv_sem=entering_sem(u, me),
            device_id=at_plane(p),
            device_id_type=MESH,
        )

    def last_entering(p):
        u = PARTS - 1
        return pltpu.make_async_remote_copy(
            src_ref=ready.at[u, p],
            dst_ref=entering.at[(u // 2) * XY + p, u % 2],
            send_sem=os_sem.at[u],
            recv_sem=entering_sem(u, p),
            device_id=at_plane(p),
            device_id_type=MESH,
        )

    def all_entering(u):
        block = ready.at[u, pl.ds(0, XY - 1)]
        return pltpu.make_async_remote_copy(
            src_ref=block,
            dst_ref=block,
            send_sem=os_sem.at[u],
            recv_sem=or_sem.at[min(u, PARTS - 2)],
            device_id=partner,
            device_id_type=MESH,
        )

    def make_entering(j):
        all_z(j).wait_recv()
        start = (jnp.zeros((HALF, HD), F32), jnp.zeros((HALF, HD), F32))
        for n in range(1, Z):
            t = z_step(n)
            got = zgot[j, t]
            start = (start[0] + tab_z[0, t] * got, start[1] + tab_z[1, t] * got)

        def step(p, carry):
            a, b = carry
            r = XY - 1 - p
            ready[j, p, 0] = (tab_p[1, p] * a).astype(BF16)
            ready[j, r, 1] = (tab_p[3, r] * b).astype(BF16)
            a = tab_p[0, p] * a + arrived[j, p, 0].astype(F32)
            b = tab_p[2, r] * b + arrived[j, r, 1].astype(F32)
            return a, b

        lax.fori_loop(0, XY, step, start)
        entering[(j // 2) * XY + me, j % 2] = ready[j, me]

        for i in range(1, XY):
            send_entering(j, i).start()

    def finish(j):
        last = j == CHUNKS - 1
        all_entering(2 * j).wait_recv()
        if not last:
            all_entering(2 * j + 1).wait_recv()

        def step(i, carry):
            p = behind(i)
            h = j * XY + p

            if last:

                @pl.when(i > 0)
                def _():
                    last_entering(p).wait_recv()

            a = entering[h, :, 0].reshape(HD, HD)
            b = entering[h, :, 1].reshape(HD, HD)
            dq = part[0, h] + mask_f[1] * dot(tok(3, h), a, 1, 0)
            dk = part[1, h] + mask_f[2] * dot(tok(2, h), b, 1, 0)
            dv = part[2, h] + mask_f[2] * dot(tok(1, h), b, 1, 1)
            outs[0, h] = dq.astype(BF16).reshape(2, TK, HD)
            outs[1, h] = dk.astype(BF16).reshape(2, TK, HD)
            outs[2, h] = dv.astype(BF16).reshape(2, TK, HD)
            return carry

        lax.fori_loop(0, XY, step, 0)

    def swap_out(j, a, core):
        swapped[a, j, core] = jnp.swapaxes(outs[a, pl.ds(j * XY, XY), core], 0, 1)

    def out_own(j, a):
        return pltpu.make_async_copy(
            swapped.at[a, j, c],
            out_refs[a].at[:, pl.ds(pl.multiple_of(c * NH + j * XY, 8), XY)],
            yl_sem.at[j, a],
        )

    def out_core(j, a):
        return pltpu.make_async_remote_copy(
            src_ref=swapped.at[a, j, other],
            dst_ref=out_refs[a].at[:, pl.ds(pl.multiple_of(c * NH + j * XY, 8), XY)],
            send_sem=ys_sem.at[j, a],
            recv_sem=yr_sem.at[j, a],
            device_id=partner,
            device_id_type=MESH,
        )

    def out_arrival(j, a):
        return pltpu.make_async_remote_copy(
            src_ref=swapped.at[a, j, other],
            dst_ref=out_refs[a].at[:, pl.ds(pl.multiple_of(other * NH + j * XY, 8), XY)],
            send_sem=ys_sem.at[j, a],
            recv_sem=yr_sem.at[j, a],
            device_id=partner,
            device_id_type=MESH,
        )

    for j in range(CHUNKS):
        for a in range(4):
            own_copy(j, a).wait()
        swap_in(j, c)
    pl.semaphore_wait(barrier, XY + Z - 1)
    for j in range(CHUNKS):
        for a in range(4):
            core_copy(j, a).start()
    for j in range(CHUNKS):
        for a in range(4):
            core_arrival(j, a).wait_recv()
        swap_in(j, other)
        make_sums(j)
    lax.fori_loop(0, XY, fill_plane, 0)
    lax.fori_loop(0, Z, fill_z, 0)

    def gather(u):
        plane_totals(u)
        send_totals(u)

    piece = NH // PARTS
    for u in range(PARTS):
        local_work(u * piece, (u + 1) * piece)
        gather(u)
        if u >= 2:
            make_entering(u - 2)
    make_entering(PARTS - 2)
    make_entering(PARTS - 1)
    for j in range(CHUNKS):
        for a in range(4):
            core_copy(j, a).wait_send()
    for u in range(PARTS):
        all_sums(u).wait_send()
        all_z(u).wait_send()
    for j in range(CHUNKS):
        finish(j)
        for a in range(3):
            swap_out(j, a, other)
            out_core(j, a).start()
        for a in range(3):
            swap_out(j, a, c)
            out_own(j, a).start()

    for u in range(PARTS):
        all_entering(u).wait_send()
    for j in range(CHUNKS):
        for a in range(3):
            out_own(j, a).wait()
            out_core(j, a).wait_send()
            out_arrival(j, a).wait_recv()


def exchange(dims, scaling, lengths, q, k, v, g):
    Z, Y, X, NH, TK = dims
    XY = X * Y
    CHUNKS = NH // XY
    CT = 2 * TK
    PARTS = 2 * CHUNKS
    HALF = HD // 2
    shape = jax.ShapeDtypeStruct((TK, 2 * NH, HD), BF16)
    dma = pltpu.SemaphoreType.DMA
    return pl.pallas_call(
        functools.partial(kernel, dims, scaling),
        out_shape=(shape, shape, shape),
        in_specs=[pl.BlockSpec(memory_space=pltpu.SMEM)] + [pl.BlockSpec(memory_space=pl.ANY)] * 4,
        out_specs=(pl.BlockSpec(memory_space=pl.ANY),) * 3,
        scratch_shapes=[
            pltpu.VMEM((4, CHUNKS, 2, TK, XY, HD), BF16),
            pltpu.VMEM((4, NH, 2, TK, HD), BF16),
            pltpu.VMEM((NH, 2, 2, HALF, HD), BF16),
            pltpu.VMEM((PARTS, XY, 2, HALF, HD), BF16),
            pltpu.VMEM((PARTS, 2, HALF, HD), F32),
            pltpu.VMEM((PARTS, Z, HALF, HD), F32),
            pltpu.VMEM((PARTS, XY, 2, HALF, HD), BF16),
            pltpu.VMEM((NH, 2, 2, HALF, HD), BF16),
            pltpu.VMEM((3, NH, CT, HD), F32),
            pltpu.VMEM((3, NH, 2, TK, HD), BF16),
            pltpu.VMEM((3, CHUNKS, 2, TK, XY, HD), BF16),
            pltpu.VMEM((3, CT, HD), F32),
            pltpu.VMEM((2, CT, HD), BF16),
            pltpu.SMEM((NDOC,), jnp.int32),
            pltpu.SMEM((4, XY), F32),
            pltpu.SMEM((2, Z), F32),
            dma((CHUNKS, 4)),
            dma((CHUNKS, 4)),
            dma((CHUNKS, 4)),
            dma((PARTS,)),
            dma((PARTS,)),
            dma((PARTS,)),
            dma((PARTS,)),
            dma((PARTS,)),
            dma((PARTS - 1,)),
            dma((XY,)),
            dma((CHUNKS, 3)),
            dma((CHUNKS, 3)),
            dma((CHUNKS, 3)),
        ],
        compiler_params=pltpu.CompilerParams(
            collective_id=0, has_side_effects=True, vmem_limit_bytes=56 << 20
        ),
    )(lengths, q, k, v, g)


def store_kernel(a_ref, b_ref, c_ref, oa_ref, ob_ref, oc_ref, sems):
    pairs = ((a_ref, oa_ref), (b_ref, ob_ref), (c_ref, oc_ref))
    copies = [pltpu.make_async_copy(i, o, sems.at[n]) for n, (i, o) in enumerate(pairs)]
    for copy in copies:
        copy.start()
    for copy in copies:
        copy.wait()


def store(results):
    shape = jax.ShapeDtypeStruct(results[0].shape, BF16)
    return pl.pallas_call(
        store_kernel,
        out_shape=(shape,) * 3,
        in_specs=[pl.BlockSpec(memory_space=pltpu.VMEM)] * 3,
        out_specs=(pl.BlockSpec(memory_space=pl.ANY),) * 3,
        scratch_shapes=[pltpu.SemaphoreType.DMA((3,))],
    )(*results)


def build(mesh, Z, Y, X):
    def local(queries, key_heads, value_heads, grad_output, doc_lengths):
        tokens, heads, width = queries.shape
        all_tokens = tokens * Z * Y * X * 2
        scaling = 1.0 / math.sqrt(width * (all_tokens // 2))
        dims = (Z, Y, X, heads // 2, tokens)
        return store(exchange(dims, scaling, doc_lengths, queries, key_heads, value_heads, grad_output))

    placed = P(("seq", "head"), None, None)
    return jax.shard_map(
        local,
        mesh=mesh,
        in_specs=(placed,) * 4 + (P(),),
        out_specs=(placed,) * 3,
        check_vma=False,
    )


def solution(mesh):
    return build(mesh, mesh.shape["seq"] // 4, 4, mesh.shape["head"] // 2)
```

```python
import functools
import math

import jax
import jax.numpy as jnp
from jax import lax
from jax.experimental import pallas as pl
from jax.experimental.pallas import tpu as pltpu
from jax.sharding import PartitionSpec as P

MESH = pl.DeviceIdType.MESH
F32 = jnp.float32
BF16 = jnp.bfloat16
NDOC = 16
HD = 128


STEPS = (
    (0, 0), (2, 2), (0, 2), (2, 1), (0, 3), (1, 2), (3, 2), (2, 3),
    (3, 3), (1, 3), (3, 1), (2, 0), (1, 1), (3, 0), (0, 1), (1, 0),
)
STEPS_X = sum(dx << (2 * i) for i, (dx, dy) in enumerate(STEPS))
STEPS_Y = sum(dy << (2 * i) for i, (dx, dy) in enumerate(STEPS))


def dot(a, b, ca, cb):
    return lax.dot_general(a, b, (((ca,), (cb,)), ((), ())), preferred_element_type=F32)


def kernel(
    dims, scaling,
    len_hbm, q_ref, k_ref, v_ref, g_ref,
    oq_ref, ok_ref, ov_ref,
    raw, toks, sums, arrived, totals, zgot, ready, entering, part, outs, swapped, mask_f, mask_b,
    len_ref, ends, tab_p, tab_z,
    len_sem, own_sem, xs_sem, xr_sem, is_sem, ir_sem, zs_sem, zr_sem, os_sem, or_sem, last_sem, ys_sem, yr_sem, yl_sem,
):
    Z, Y, X, NH, TK = dims
    XY = X * Y
    CHUNKS = NH // XY
    PARTS = 2 * CHUNKS
    HALF = HD // 2
    CT = 2 * TK
    PT = XY * CT
    s = lax.axis_index("seq")
    hh = lax.axis_index("head")
    z, y = s // Y, s % Y
    x, c = hh // 2, hh % 2
    other = 1 - c
    me = y * X + x
    ins = (q_ref, k_ref, v_ref, g_ref)
    out_refs = (oq_ref, ok_ref, ov_ref)
    partner = (s, x * 2 + other)

    def at_plane(p):
        return (z * Y + p // X, (p % X) * 2 + c)

    def at_z(t):
        return (t * Y + y, hh)

    def plane_step(dx, dy):
        return (z * Y + (y + dy) % Y, ((x + dx) % X) * 2 + c)

    def offset(i):
        return (STEPS_X >> (2 * i)) & 3, (STEPS_Y >> (2 * i)) & 3

    def ahead(i):
        dx, dy = offset(i)
        return ((y + dy) % Y) * X + (x + dx) % X

    def behind(i):
        dx, dy = offset(i)
        return ((y - dy + Y) % Y) * X + (x - dx + X) % X

    def z_step(n):
        return (z + (((n + 1) // 2) if n % 2 else Z - n // 2)) % Z

    lengths = pltpu.make_async_copy(len_hbm, len_ref, len_sem)
    lengths.start()
    barrier = pltpu.get_barrier_semaphore()

    def greet(device):
        pl.semaphore_signal(barrier, inc=1, device_id=device, device_id_type=MESH)

    for n in range(Z - 1, 3, -1):
        greet(at_z(z_step(n)))
    for dx, dy in STEPS[1:]:
        greet(plane_step(dx, dy))
    for n in range(3, 0, -1):
        greet(at_z(z_step(n)))
    greet(partner)

    def own_copy(j, a):
        return pltpu.make_async_copy(
            ins[a].at[:, pl.ds(pl.multiple_of(c * NH + j * XY, 8), XY)],
            raw.at[a, j, c],
            own_sem.at[j, a],
        )

    def core_copy(j, a):
        return pltpu.make_async_remote_copy(
            src_ref=ins[a].at[:, pl.ds(pl.multiple_of(other * NH + j * XY, 8), XY)],
            dst_ref=raw.at[a, j, c],
            send_sem=xs_sem.at[j, a],
            recv_sem=xr_sem.at[j, a],
            device_id=partner,
            device_id_type=MESH,
        )

    def core_arrival(j, a):
        return pltpu.make_async_remote_copy(
            src_ref=ins[a].at[:, pl.ds(pl.multiple_of(other * NH + j * XY, 8), XY)],
            dst_ref=raw.at[a, j, other],
            send_sem=xs_sem.at[j, a],
            recv_sem=xr_sem.at[j, a],
            device_id=partner,
            device_id_type=MESH,
        )

    for j in range(CHUNKS):
        for a in range(4):
            own_copy(j, a).start()

    lengths.wait()
    total_len = jnp.int32(0)
    for d in range(NDOC):
        total_len = total_len + len_ref[d]
        ends[d] = total_len

    def same(low, high):
        cut = jnp.int32(0)
        for d in range(NDOC):
            e = ends[d]
            cut = cut + jnp.where((low < e) & (e <= high), 1, 0)
        return jnp.where(cut == 0, 1.0, 0.0).astype(F32)

    def fill_plane(p, carry):
        first = z * PT + p * CT
        last = first + CT - 1
        tab_p[0, p] = same(first - 1, last)
        tab_p[1, p] = same(first - 1, first)
        tab_p[2, p] = same(first, last + 1)
        tab_p[3, p] = same(last, last + 1)
        return carry

    def fill_z(t, carry):
        tab_z[0, t] = jnp.where(t < z, same((t + 1) * PT - 1, z * PT - 1), 0.0).astype(F32)
        tab_z[1, t] = jnp.where(t > z, same((z + 1) * PT, t * PT), 0.0).astype(F32)
        return carry

    base = (s * X + x) * CT
    rows = base + lax.broadcasted_iota(jnp.int32, (CT, CT), 0)
    cols = base + lax.broadcasted_iota(jnp.int32, (CT, CT), 1)
    row_doc = jnp.zeros((CT, CT), jnp.int32)
    col_doc = jnp.zeros((CT, CT), jnp.int32)
    first_doc = jnp.int32(0)
    last_doc = jnp.int32(0)
    for d in range(NDOC):
        e = ends[d]
        row_doc = row_doc + (e <= rows).astype(jnp.int32)
        col_doc = col_doc + (e <= cols).astype(jnp.int32)
        first_doc = first_doc + jnp.where(e <= base, 1, 0)
        last_doc = last_doc + jnp.where(e <= base + CT - 1, 1, 0)
    in_block = jnp.where((row_doc == col_doc) & (rows >= cols), scaling, 0.0).astype(F32)
    leading = jnp.where(row_doc == first_doc, 1.0, 0.0).astype(F32)
    trailing = jnp.where(row_doc == last_doc, 1.0, 0.0).astype(F32)
    mask_f[0] = in_block
    mask_f[1] = leading
    mask_f[2] = trailing
    mask_b[0] = leading.astype(BF16)
    mask_b[1] = trailing.astype(BF16)

    def tok(a, h):
        return toks[a, h].reshape(CT, HD)

    def swap_in(j, core):
        for a in range(4):
            toks[a, pl.ds(j * XY, XY), core] = jnp.swapaxes(raw[a, j, core], 0, 1)

    def send_sum(u, i):
        p = ahead(i)
        return pltpu.make_async_remote_copy(
            src_ref=sums.at[(u // 2) * XY + p, u % 2],
            dst_ref=arrived.at[u, me],
            send_sem=is_sem.at[u],
            recv_sem=ir_sem.at[u],
            device_id=at_plane(p),
            device_id_type=MESH,
        )

    def all_sums(u):
        block = arrived.at[u, pl.ds(0, XY - 1)]
        return pltpu.make_async_remote_copy(
            src_ref=block,
            dst_ref=block,
            send_sem=is_sem.at[u],
            recv_sem=ir_sem.at[u],
            device_id=partner,
            device_id_type=MESH,
        )

    def make_sums(j):
        def step(n, carry):
            i = n % XY
            h = j * XY + ahead(i)
            keys = tok(1, h) * mask_b[1]
            a_sum = (dot(tok(2, h), keys, 0, 0) * scaling).astype(BF16).reshape(2, HALF, HD)
            queries = tok(0, h) * mask_b[0]
            b_sum = (dot(tok(3, h), queries, 0, 0) * scaling).astype(BF16).reshape(2, HALF, HD)
            for r in range(2):
                sums[h, r, 0] = a_sum[r]
                sums[h, r, 1] = b_sum[r]

            @pl.when(i == 0)
            def _():
                for r in range(2):
                    arrived[2 * j + r, me, 0] = a_sum[r]
                    arrived[2 * j + r, me, 1] = b_sum[r]

            @pl.when(n >= 2)
            def _():
                send_sum(2 * j, n - 1).start()

            return carry

        lax.fori_loop(1, XY + 1, step, 0)

        for i in range(1, XY):
            send_sum(2 * j + 1, i).start()

    def local_work(low, high):
        def step(h, carry):
            q, k, v, g = (tok(a, h) for a in range(4))
            gs = (dot(g, v, 1, 1) * mask_f[0]).astype(BF16)
            sc = (dot(q, k, 1, 1) * mask_f[0]).astype(BF16)
            part[0, h] = dot(gs, k, 1, 0)
            part[1, h] = dot(gs, q, 0, 0)
            part[2, h] = dot(sc, g, 0, 0)
            return carry

        lax.fori_loop(low, high, step, 0)

    def z_copy(u, n):
        t = z_step(n)
        return pltpu.make_async_remote_copy(
            src_ref=totals.at[u, jnp.where(t < z, 1, 0)],
            dst_ref=zgot.at[u, z],
            send_sem=zs_sem.at[u],
            recv_sem=zr_sem.at[u],
            device_id=at_z(t),
            device_id_type=MESH,
        )

    def all_z(u):
        block = zgot.at[u, pl.ds(0, Z - 1)]
        return pltpu.make_async_remote_copy(
            src_ref=block,
            dst_ref=block,
            send_sem=zs_sem.at[u],
            recv_sem=zr_sem.at[u],
            device_id=partner,
            device_id_type=MESH,
        )

    def plane_totals(j):
        all_sums(j).wait_recv()

        def step(p, carry):
            a, b = carry
            r = XY - 1 - p
            a = tab_p[0, p] * a + arrived[j, p, 0].astype(F32)
            b = tab_p[2, r] * b + arrived[j, r, 1].astype(F32)
            return a, b

        zero = jnp.zeros((HALF, HD), F32)
        a, b = lax.fori_loop(0, XY, step, (zero, zero))
        totals[j, 0] = a
        totals[j, 1] = b

    def send_totals(j):
        for n in range(1, Z):
            z_copy(j, n).start()

    def entering_sem(u, p):
        return last_sem.at[p] if u == PARTS - 1 else or_sem.at[u]

    def send_entering(u, i):
        p = ahead(i)
        return pltpu.make_async_remote_copy(
            src_ref=ready.at[u, p],
            dst_ref=entering.at[(u // 2) * XY + me, u % 2],
            send_sem=os_sem.at[u],
            recv_sem=entering_sem(u, me),
            device_id=at_plane(p),
            device_id_type=MESH,
        )

    def last_entering(p):
        u = PARTS - 1
        return pltpu.make_async_remote_copy(
            src_ref=ready.at[u, p],
            dst_ref=entering.at[(u // 2) * XY + p, u % 2],
            send_sem=os_sem.at[u],
            recv_sem=entering_sem(u, p),
            device_id=at_plane(p),
            device_id_type=MESH,
        )

    def all_entering(u):
        block = ready.at[u, pl.ds(0, XY - 1)]
        return pltpu.make_async_remote_copy(
            src_ref=block,
            dst_ref=block,
            send_sem=os_sem.at[u],
            recv_sem=or_sem.at[min(u, PARTS - 2)],
            device_id=partner,
            device_id_type=MESH,
        )

    def make_entering(j):
        all_z(j).wait_recv()
        start = (jnp.zeros((HALF, HD), F32), jnp.zeros((HALF, HD), F32))
        for n in range(1, Z):
            t = z_step(n)
            got = zgot[j, t]
            start = (start[0] + tab_z[0, t] * got, start[1] + tab_z[1, t] * got)

        def step(p, carry):
            a, b = carry
            r = XY - 1 - p
            ready[j, p, 0] = (tab_p[1, p] * a).astype(BF16)
            ready[j, r, 1] = (tab_p[3, r] * b).astype(BF16)
            a = tab_p[0, p] * a + arrived[j, p, 0].astype(F32)
            b = tab_p[2, r] * b + arrived[j, r, 1].astype(F32)
            return a, b

        lax.fori_loop(0, XY, step, start)
        entering[(j // 2) * XY + me, j % 2] = ready[j, me]

        for i in range(1, XY):
            send_entering(j, i).start()

    def finish(j):
        last = j == CHUNKS - 1
        all_entering(2 * j).wait_recv()
        if not last:
            all_entering(2 * j + 1).wait_recv()

        def step(i, carry):
            p = behind(i)
            h = j * XY + p

            if last:

                @pl.when(i > 0)
                def _():
                    last_entering(p).wait_recv()

            a = entering[h, :, 0].reshape(HD, HD)
            b = entering[h, :, 1].reshape(HD, HD)
            dq = part[0, h] + mask_f[1] * dot(tok(3, h), a, 1, 0)
            dk = part[1, h] + mask_f[2] * dot(tok(2, h), b, 1, 0)
            dv = part[2, h] + mask_f[2] * dot(tok(1, h), b, 1, 1)
            outs[0, h] = dq.astype(BF16).reshape(2, TK, HD)
            outs[1, h] = dk.astype(BF16).reshape(2, TK, HD)
            outs[2, h] = dv.astype(BF16).reshape(2, TK, HD)
            return carry

        lax.fori_loop(0, XY, step, 0)

    def swap_out(j, a, core):
        swapped[a, j, core] = jnp.swapaxes(outs[a, pl.ds(j * XY, XY), core], 0, 1)

    def out_own(j, a):
        return pltpu.make_async_copy(
            swapped.at[a, j, c],
            out_refs[a].at[:, pl.ds(pl.multiple_of(c * NH + j * XY, 8), XY)],
            yl_sem.at[j, a],
        )

    def out_core(j, a):
        return pltpu.make_async_remote_copy(
            src_ref=swapped.at[a, j, other],
            dst_ref=out_refs[a].at[:, pl.ds(pl.multiple_of(c * NH + j * XY, 8), XY)],
            send_sem=ys_sem.at[j, a],
            recv_sem=yr_sem.at[j, a],
            device_id=partner,
            device_id_type=MESH,
        )

    def out_arrival(j, a):
        return pltpu.make_async_remote_copy(
            src_ref=swapped.at[a, j, other],
            dst_ref=out_refs[a].at[:, pl.ds(pl.multiple_of(other * NH + j * XY, 8), XY)],
            send_sem=ys_sem.at[j, a],
            recv_sem=yr_sem.at[j, a],
            device_id=partner,
            device_id_type=MESH,
        )

    for j in range(CHUNKS):
        for a in range(4):
            own_copy(j, a).wait()
        swap_in(j, c)
    pl.semaphore_wait(barrier, XY + Z - 1)
    for j in range(CHUNKS):
        for a in range(4):
            core_copy(j, a).start()
    for j in range(CHUNKS):
        for a in range(4):
            core_arrival(j, a).wait_recv()
        swap_in(j, other)
        make_sums(j)
    lax.fori_loop(0, XY, fill_plane, 0)
    lax.fori_loop(0, Z, fill_z, 0)

    def gather(u):
        plane_totals(u)
        send_totals(u)

    piece = NH // PARTS
    for u in range(PARTS):
        local_work(u * piece, (u + 1) * piece)
        gather(u)
        if u >= 2:
            make_entering(u - 2)
    make_entering(PARTS - 2)
    make_entering(PARTS - 1)
    for j in range(CHUNKS):
        for a in range(4):
            core_copy(j, a).wait_send()
    for u in range(PARTS):
        all_sums(u).wait_send()
        all_z(u).wait_send()
    for j in range(CHUNKS):
        finish(j)
        for a in range(3):
            swap_out(j, a, other)
            out_core(j, a).start()
        for a in range(3):
            swap_out(j, a, c)
            out_own(j, a).start()

    for u in range(PARTS):
        all_entering(u).wait_send()
    for j in range(CHUNKS):
        for a in range(3):
            out_own(j, a).wait()
            out_core(j, a).wait_send()
            out_arrival(j, a).wait_recv()


def exchange(dims, scaling, lengths, q, k, v, g):
    Z, Y, X, NH, TK = dims
    XY = X * Y
    CHUNKS = NH // XY
    CT = 2 * TK
    PARTS = 2 * CHUNKS
    HALF = HD // 2
    shape = jax.ShapeDtypeStruct((TK, 2 * NH, HD), BF16)
    dma = pltpu.SemaphoreType.DMA
    return pl.pallas_call(
        functools.partial(kernel, dims, scaling),
        out_shape=(shape, shape, shape),
        in_specs=[pl.BlockSpec(memory_space=pl.ANY)] * 5,
        out_specs=(pl.BlockSpec(memory_space=pl.ANY),) * 3,
        scratch_shapes=[
            pltpu.VMEM((4, CHUNKS, 2, TK, XY, HD), BF16),
            pltpu.VMEM((4, NH, 2, TK, HD), BF16),
            pltpu.VMEM((NH, 2, 2, HALF, HD), BF16),
            pltpu.VMEM((PARTS, XY, 2, HALF, HD), BF16),
            pltpu.VMEM((PARTS, 2, HALF, HD), F32),
            pltpu.VMEM((PARTS, Z, HALF, HD), F32),
            pltpu.VMEM((PARTS, XY, 2, HALF, HD), BF16),
            pltpu.VMEM((NH, 2, 2, HALF, HD), BF16),
            pltpu.VMEM((3, NH, CT, HD), F32),
            pltpu.VMEM((3, NH, 2, TK, HD), BF16),
            pltpu.VMEM((3, CHUNKS, 2, TK, XY, HD), BF16),
            pltpu.VMEM((3, CT, HD), F32),
            pltpu.VMEM((2, CT, HD), BF16),
            pltpu.SMEM((NDOC,), jnp.int32),
            pltpu.SMEM((NDOC,), jnp.int32),
            pltpu.SMEM((4, XY), F32),
            pltpu.SMEM((2, Z), F32),
            dma,
            dma((CHUNKS, 4)),
            dma((CHUNKS, 4)),
            dma((CHUNKS, 4)),
            dma((PARTS,)),
            dma((PARTS,)),
            dma((PARTS,)),
            dma((PARTS,)),
            dma((PARTS,)),
            dma((PARTS - 1,)),
            dma((XY,)),
            dma((CHUNKS, 3)),
            dma((CHUNKS, 3)),
            dma((CHUNKS, 3)),
        ],
        compiler_params=pltpu.CompilerParams(
            collective_id=0, has_side_effects=True, vmem_limit_bytes=56 << 20
        ),
    )(lengths, q, k, v, g)


PIECES = 4


def store_kernel(a_ref, b_ref, c_ref, oa_ref, ob_ref, oc_ref, held, in_sems, out_sems):
    size = a_ref.shape[0] // PIECES
    loads, stores = [], []
    for n, (source, target) in enumerate(((a_ref, oa_ref), (b_ref, ob_ref), (c_ref, oc_ref))):
        for m in range(PIECES):
            rows = pl.ds(m * size, size)
            loads.append(pltpu.make_async_copy(source.at[rows], held.at[n, rows], in_sems.at[n, m]))
            stores.append(pltpu.make_async_copy(held.at[n, rows], target.at[rows], out_sems.at[n, m]))
    for load in loads:
        load.start()
    for load, store_piece in zip(loads, stores):
        load.wait()
        store_piece.start()
    for store_piece in stores:
        store_piece.wait()


def store(results):
    shape = jax.ShapeDtypeStruct(results[0].shape, BF16)
    return pl.pallas_call(
        store_kernel,
        out_shape=(shape,) * 3,
        in_specs=[pl.BlockSpec(memory_space=pl.ANY)] * 3,
        out_specs=(pl.BlockSpec(memory_space=pl.ANY),) * 3,
        scratch_shapes=[
            pltpu.VMEM((3,) + results[0].shape, BF16),
            pltpu.SemaphoreType.DMA((3, PIECES)),
            pltpu.SemaphoreType.DMA((3, PIECES)),
        ],
    )(*results)


def build(mesh, Z, Y, X):
    def local(queries, key_heads, value_heads, grad_output, doc_lengths):
        tokens, heads, width = queries.shape
        all_tokens = tokens * Z * Y * X * 2
        scaling = 1.0 / math.sqrt(width * (all_tokens // 2))
        dims = (Z, Y, X, heads // 2, tokens)
        return store(exchange(dims, scaling, doc_lengths, queries, key_heads, value_heads, grad_output))

    placed = P(("seq", "head"), None, None)
    return jax.shard_map(
        local,
        mesh=mesh,
        in_specs=(placed,) * 4 + (P(),),
        out_specs=(placed,) * 3,
        check_vma=False,
    )


def solution(mesh):
    return build(mesh, mesh.shape["seq"] // 4, 4, mesh.shape["head"] // 2)
```

```python
import functools
import math

import jax
import jax.numpy as jnp
from jax import lax
from jax.experimental import pallas as pl
from jax.experimental.pallas import tpu as pltpu
from jax.sharding import PartitionSpec as P

MESH = pl.DeviceIdType.MESH
F32 = jnp.float32
BF16 = jnp.bfloat16
NDOC = 16
HD = 128


STEPS = (
    (0, 0), (2, 2), (0, 2), (2, 1), (0, 3), (1, 2), (3, 2), (2, 3),
    (3, 3), (1, 3), (3, 1), (2, 0), (1, 1), (3, 0), (0, 1), (1, 0),
)
STEPS_X = sum(dx << (2 * i) for i, (dx, dy) in enumerate(STEPS))
STEPS_Y = sum(dy << (2 * i) for i, (dx, dy) in enumerate(STEPS))


def dot(a, b, ca, cb):
    return lax.dot_general(a, b, (((ca,), (cb,)), ((), ())), preferred_element_type=F32)


def kernel(
    dims, scaling,
    len_hbm, q_ref, k_ref, v_ref, g_ref,
    oq_ref, ok_ref, ov_ref,
    raw, toks, sums, arrived, totals, zgot, ready, entering, part, outs, swapped, mask_f, mask_b,
    len_ref, ends, tab_p, tab_z,
    len_sem, own_sem, xs_sem, xr_sem, is_sem, ir_sem, zs_sem, zr_sem, os_sem, or_sem, last_sem, ys_sem, yr_sem, yl_sem,
):
    Z, Y, X, NH, TK = dims
    XY = X * Y
    CHUNKS = NH // XY
    PARTS = 2 * CHUNKS
    HALF = HD // 2
    CT = 2 * TK
    PT = XY * CT
    s = lax.axis_index("seq")
    hh = lax.axis_index("head")
    z, y = s // Y, s % Y
    x, c = hh // 2, hh % 2
    other = 1 - c
    me = y * X + x
    ins = (q_ref, k_ref, v_ref, g_ref)
    out_refs = (oq_ref, ok_ref, ov_ref)
    partner = (s, x * 2 + other)

    def at_plane(p):
        return (z * Y + p // X, (p % X) * 2 + c)

    def at_z(t):
        return (t * Y + y, hh)

    def plane_step(dx, dy):
        return (z * Y + (y + dy) % Y, ((x + dx) % X) * 2 + c)

    def offset(i):
        return (STEPS_X >> (2 * i)) & 3, (STEPS_Y >> (2 * i)) & 3

    def ahead(i):
        dx, dy = offset(i)
        return ((y + dy) % Y) * X + (x + dx) % X

    def behind(i):
        dx, dy = offset(i)
        return ((y - dy + Y) % Y) * X + (x - dx + X) % X

    def z_step(n):
        return (z + (((n + 1) // 2) if n % 2 else Z - n // 2)) % Z

    lengths = pltpu.make_async_copy(len_hbm, len_ref, len_sem)
    lengths.start()
    barrier = pltpu.get_barrier_semaphore()

    def greet(device):
        pl.semaphore_signal(barrier, inc=1, device_id=device, device_id_type=MESH)

    for n in range(Z - 1, 3, -1):
        greet(at_z(z_step(n)))
    for dx, dy in STEPS[1:]:
        greet(plane_step(dx, dy))
    for n in range(3, 0, -1):
        greet(at_z(z_step(n)))
    greet(partner)

    def own_copy(j, a):
        return pltpu.make_async_copy(
            ins[a].at[:, pl.ds(pl.multiple_of(c * NH + j * XY, 8), XY)],
            raw.at[a, j, c],
            own_sem.at[j, a],
        )

    def core_copy(j, a):
        return pltpu.make_async_remote_copy(
            src_ref=ins[a].at[:, pl.ds(pl.multiple_of(other * NH + j * XY, 8), XY)],
            dst_ref=raw.at[a, j, c],
            send_sem=xs_sem.at[j, a],
            recv_sem=xr_sem.at[j, a],
            device_id=partner,
            device_id_type=MESH,
        )

    def core_arrival(j, a):
        return pltpu.make_async_remote_copy(
            src_ref=ins[a].at[:, pl.ds(pl.multiple_of(other * NH + j * XY, 8), XY)],
            dst_ref=raw.at[a, j, other],
            send_sem=xs_sem.at[j, a],
            recv_sem=xr_sem.at[j, a],
            device_id=partner,
            device_id_type=MESH,
        )

    for j in range(CHUNKS):
        for a in range(4):
            own_copy(j, a).start()

    lengths.wait()
    total_len = jnp.int32(0)
    for d in range(NDOC):
        total_len = total_len + len_ref[d]
        ends[d] = total_len

    def same(low, high):
        cut = jnp.int32(0)
        for d in range(NDOC):
            e = ends[d]
            cut = cut + jnp.where((low < e) & (e <= high), 1, 0)
        return jnp.where(cut == 0, 1.0, 0.0).astype(F32)

    def fill_plane(p, carry):
        first = z * PT + p * CT
        last = first + CT - 1
        tab_p[0, p] = same(first - 1, last)
        tab_p[1, p] = same(first - 1, first)
        tab_p[2, p] = same(first, last + 1)
        tab_p[3, p] = same(last, last + 1)
        return carry

    def fill_z(t, carry):
        tab_z[0, t] = jnp.where(t < z, same((t + 1) * PT - 1, z * PT - 1), 0.0).astype(F32)
        tab_z[1, t] = jnp.where(t > z, same((z + 1) * PT, t * PT), 0.0).astype(F32)
        return carry

    base = (s * X + x) * CT
    rows = base + lax.broadcasted_iota(jnp.int32, (CT, CT), 0)
    cols = base + lax.broadcasted_iota(jnp.int32, (CT, CT), 1)
    row_doc = jnp.zeros((CT, CT), jnp.int32)
    col_doc = jnp.zeros((CT, CT), jnp.int32)
    first_doc = jnp.int32(0)
    last_doc = jnp.int32(0)
    for d in range(NDOC):
        e = ends[d]
        row_doc = row_doc + (e <= rows).astype(jnp.int32)
        col_doc = col_doc + (e <= cols).astype(jnp.int32)
        first_doc = first_doc + jnp.where(e <= base, 1, 0)
        last_doc = last_doc + jnp.where(e <= base + CT - 1, 1, 0)
    in_block = jnp.where((row_doc == col_doc) & (rows >= cols), scaling, 0.0).astype(F32)
    leading = jnp.where(row_doc == first_doc, 1.0, 0.0).astype(F32)
    trailing = jnp.where(row_doc == last_doc, 1.0, 0.0).astype(F32)
    mask_f[0] = in_block
    mask_f[1] = leading
    mask_f[2] = trailing
    mask_b[0] = leading.astype(BF16)
    mask_b[1] = trailing.astype(BF16)

    def tok(a, h):
        return toks[a, h].reshape(CT, HD)

    def swap_in(j, core):
        for a in range(4):
            toks[a, pl.ds(j * XY, XY), core] = jnp.swapaxes(raw[a, j, core], 0, 1)

    def send_sum(u, i):
        p = ahead(i)
        return pltpu.make_async_remote_copy(
            src_ref=sums.at[(u // 2) * XY + p, u % 2],
            dst_ref=arrived.at[u, me],
            send_sem=is_sem.at[u],
            recv_sem=ir_sem.at[u],
            device_id=at_plane(p),
            device_id_type=MESH,
        )

    def all_sums(u):
        block = arrived.at[u, pl.ds(0, XY - 1)]
        return pltpu.make_async_remote_copy(
            src_ref=block,
            dst_ref=block,
            send_sem=is_sem.at[u],
            recv_sem=ir_sem.at[u],
            device_id=partner,
            device_id_type=MESH,
        )

    def make_sums(j):
        def step(n, carry):
            i = n % XY
            h = j * XY + ahead(i)
            keys = tok(1, h) * mask_b[1]
            a_sum = (dot(tok(2, h), keys, 0, 0) * scaling).astype(BF16).reshape(2, HALF, HD)
            queries = tok(0, h) * mask_b[0]
            b_sum = (dot(tok(3, h), queries, 0, 0) * scaling).astype(BF16).reshape(2, HALF, HD)
            for r in range(2):
                sums[h, r, 0] = a_sum[r]
                sums[h, r, 1] = b_sum[r]

            @pl.when(i == 0)
            def _():
                for r in range(2):
                    arrived[2 * j + r, me, 0] = a_sum[r]
                    arrived[2 * j + r, me, 1] = b_sum[r]

            @pl.when(n >= 2)
            def _():
                send_sum(2 * j, n - 1).start()

            return carry

        lax.fori_loop(1, XY + 1, step, 0, unroll=2)

        for i in range(1, XY):
            send_sum(2 * j + 1, i).start()

    def local_work(low, high):
        def step(h, carry):
            q, k, v, g = (tok(a, h) for a in range(4))
            gs = (dot(g, v, 1, 1) * mask_f[0]).astype(BF16)
            sc = (dot(q, k, 1, 1) * mask_f[0]).astype(BF16)
            part[0, h] = dot(gs, k, 1, 0)
            part[1, h] = dot(gs, q, 0, 0)
            part[2, h] = dot(sc, g, 0, 0)
            return carry

        lax.fori_loop(low, high, step, 0)

    def z_copy(u, n):
        t = z_step(n)
        return pltpu.make_async_remote_copy(
            src_ref=totals.at[u, jnp.where(t < z, 1, 0)],
            dst_ref=zgot.at[u, z],
            send_sem=zs_sem.at[u],
            recv_sem=zr_sem.at[u],
            device_id=at_z(t),
            device_id_type=MESH,
        )

    def all_z(u):
        block = zgot.at[u, pl.ds(0, Z - 1)]
        return pltpu.make_async_remote_copy(
            src_ref=block,
            dst_ref=block,
            send_sem=zs_sem.at[u],
            recv_sem=zr_sem.at[u],
            device_id=partner,
            device_id_type=MESH,
        )

    def plane_totals(j):
        all_sums(j).wait_recv()

        def step(p, carry):
            a, b = carry
            r = XY - 1 - p
            a = tab_p[0, p] * a + arrived[j, p, 0].astype(F32)
            b = tab_p[2, r] * b + arrived[j, r, 1].astype(F32)
            return a, b

        zero = jnp.zeros((HALF, HD), F32)
        a, b = lax.fori_loop(0, XY, step, (zero, zero), unroll=4)
        totals[j, 0] = a
        totals[j, 1] = b

    def send_totals(j):
        for n in range(1, Z):
            z_copy(j, n).start()

    def entering_sem(u, p):
        return last_sem.at[p] if u == PARTS - 1 else or_sem.at[u]

    def send_entering(u, i):
        p = ahead(i)
        return pltpu.make_async_remote_copy(
            src_ref=ready.at[u, p],
            dst_ref=entering.at[(u // 2) * XY + me, u % 2],
            send_sem=os_sem.at[u],
            recv_sem=entering_sem(u, me),
            device_id=at_plane(p),
            device_id_type=MESH,
        )

    def last_entering(p):
        u = PARTS - 1
        return pltpu.make_async_remote_copy(
            src_ref=ready.at[u, p],
            dst_ref=entering.at[(u // 2) * XY + p, u % 2],
            send_sem=os_sem.at[u],
            recv_sem=entering_sem(u, p),
            device_id=at_plane(p),
            device_id_type=MESH,
        )

    def all_entering(u):
        block = ready.at[u, pl.ds(0, XY - 1)]
        return pltpu.make_async_remote_copy(
            src_ref=block,
            dst_ref=block,
            send_sem=os_sem.at[u],
            recv_sem=or_sem.at[min(u, PARTS - 2)],
            device_id=partner,
            device_id_type=MESH,
        )

    def make_entering(j):
        all_z(j).wait_recv()
        start = (jnp.zeros((HALF, HD), F32), jnp.zeros((HALF, HD), F32))
        for n in range(1, Z):
            t = z_step(n)
            got = zgot[j, t]
            start = (start[0] + tab_z[0, t] * got, start[1] + tab_z[1, t] * got)

        def step(p, carry):
            a, b = carry
            r = XY - 1 - p
            ready[j, p, 0] = (tab_p[1, p] * a).astype(BF16)
            ready[j, r, 1] = (tab_p[3, r] * b).astype(BF16)
            a = tab_p[0, p] * a + arrived[j, p, 0].astype(F32)
            b = tab_p[2, r] * b + arrived[j, r, 1].astype(F32)
            return a, b

        lax.fori_loop(0, XY, step, start, unroll=4)
        entering[(j // 2) * XY + me, j % 2] = ready[j, me]

        for i in range(1, XY):
            send_entering(j, i).start()

    def finish(j):
        last = j == CHUNKS - 1
        all_entering(2 * j).wait_recv()
        if not last:
            all_entering(2 * j + 1).wait_recv()

        def step(i, carry):
            p = behind(i)
            h = j * XY + p

            if last:

                @pl.when(i > 0)
                def _():
                    last_entering(p).wait_recv()

            a = entering[h, :, 0].reshape(HD, HD)
            b = entering[h, :, 1].reshape(HD, HD)
            dq = part[0, h] + mask_f[1] * dot(tok(3, h), a, 1, 0)
            dk = part[1, h] + mask_f[2] * dot(tok(2, h), b, 1, 0)
            dv = part[2, h] + mask_f[2] * dot(tok(1, h), b, 1, 1)
            outs[0, h] = dq.astype(BF16).reshape(2, TK, HD)
            outs[1, h] = dk.astype(BF16).reshape(2, TK, HD)
            outs[2, h] = dv.astype(BF16).reshape(2, TK, HD)
            return carry

        lax.fori_loop(0, XY, step, 0, unroll=2)

    def swap_out(j, a, core):
        swapped[a, j, core] = jnp.swapaxes(outs[a, pl.ds(j * XY, XY), core], 0, 1)

    def out_own(j, a):
        return pltpu.make_async_copy(
            swapped.at[a, j, c],
            out_refs[a].at[:, pl.ds(pl.multiple_of(c * NH + j * XY, 8), XY)],
            yl_sem.at[j, a],
        )

    def out_core(j, a):
        return pltpu.make_async_remote_copy(
            src_ref=swapped.at[a, j, other],
            dst_ref=out_refs[a].at[:, pl.ds(pl.multiple_of(c * NH + j * XY, 8), XY)],
            send_sem=ys_sem.at[j, a],
            recv_sem=yr_sem.at[j, a],
            device_id=partner,
            device_id_type=MESH,
        )

    def out_arrival(j, a):
        return pltpu.make_async_remote_copy(
            src_ref=swapped.at[a, j, other],
            dst_ref=out_refs[a].at[:, pl.ds(pl.multiple_of(other * NH + j * XY, 8), XY)],
            send_sem=ys_sem.at[j, a],
            recv_sem=yr_sem.at[j, a],
            device_id=partner,
            device_id_type=MESH,
        )

    for j in range(CHUNKS):
        for a in range(4):
            own_copy(j, a).wait()
        swap_in(j, c)
    pl.semaphore_wait(barrier, XY + Z - 1)
    for j in range(CHUNKS):
        for a in range(4):
            core_copy(j, a).start()
    for j in range(CHUNKS):
        for a in range(4):
            core_arrival(j, a).wait_recv()
        swap_in(j, other)
        make_sums(j)
    lax.fori_loop(0, XY, fill_plane, 0)
    lax.fori_loop(0, Z, fill_z, 0)

    def gather(u):
        plane_totals(u)
        send_totals(u)

    piece = NH // PARTS
    for u in range(PARTS):
        local_work(u * piece, (u + 1) * piece)
        gather(u)
        if u >= 2:
            make_entering(u - 2)
    make_entering(PARTS - 2)
    make_entering(PARTS - 1)
    for j in range(CHUNKS):
        for a in range(4):
            core_copy(j, a).wait_send()
    for u in range(PARTS):
        all_sums(u).wait_send()
        all_z(u).wait_send()
    for j in range(CHUNKS):
        finish(j)
        for a in range(3):
            swap_out(j, a, other)
            out_core(j, a).start()
        for a in range(3):
            swap_out(j, a, c)
            out_own(j, a).start()

    for u in range(PARTS):
        all_entering(u).wait_send()
    for j in range(CHUNKS):
        for a in range(3):
            out_own(j, a).wait()
            out_core(j, a).wait_send()
            out_arrival(j, a).wait_recv()


def exchange(dims, scaling, lengths, q, k, v, g):
    Z, Y, X, NH, TK = dims
    XY = X * Y
    CHUNKS = NH // XY
    CT = 2 * TK
    PARTS = 2 * CHUNKS
    HALF = HD // 2
    shape = jax.ShapeDtypeStruct((TK, 2 * NH, HD), BF16)
    dma = pltpu.SemaphoreType.DMA
    return pl.pallas_call(
        functools.partial(kernel, dims, scaling),
        out_shape=(shape, shape, shape),
        in_specs=[pl.BlockSpec(memory_space=pl.ANY)] * 5,
        out_specs=(pl.BlockSpec(memory_space=pl.ANY),) * 3,
        scratch_shapes=[
            pltpu.VMEM((4, CHUNKS, 2, TK, XY, HD), BF16),
            pltpu.VMEM((4, NH, 2, TK, HD), BF16),
            pltpu.VMEM((NH, 2, 2, HALF, HD), BF16),
            pltpu.VMEM((PARTS, XY, 2, HALF, HD), BF16),
            pltpu.VMEM((PARTS, 2, HALF, HD), F32),
            pltpu.VMEM((PARTS, Z, HALF, HD), F32),
            pltpu.VMEM((PARTS, XY, 2, HALF, HD), BF16),
            pltpu.VMEM((NH, 2, 2, HALF, HD), BF16),
            pltpu.VMEM((3, NH, CT, HD), F32),
            pltpu.VMEM((3, NH, 2, TK, HD), BF16),
            pltpu.VMEM((3, CHUNKS, 2, TK, XY, HD), BF16),
            pltpu.VMEM((3, CT, HD), F32),
            pltpu.VMEM((2, CT, HD), BF16),
            pltpu.SMEM((NDOC,), jnp.int32),
            pltpu.SMEM((NDOC,), jnp.int32),
            pltpu.SMEM((4, XY), F32),
            pltpu.SMEM((2, Z), F32),
            dma,
            dma((CHUNKS, 4)),
            dma((CHUNKS, 4)),
            dma((CHUNKS, 4)),
            dma((PARTS,)),
            dma((PARTS,)),
            dma((PARTS,)),
            dma((PARTS,)),
            dma((PARTS,)),
            dma((PARTS - 1,)),
            dma((XY,)),
            dma((CHUNKS, 3)),
            dma((CHUNKS, 3)),
            dma((CHUNKS, 3)),
        ],
        compiler_params=pltpu.CompilerParams(
            collective_id=0, has_side_effects=True, vmem_limit_bytes=50 << 20
        ),
    )(lengths, q, k, v, g)


def store_kernel(a_ref, b_ref, c_ref, oa_ref, ob_ref, oc_ref, sems):
    pairs = ((a_ref, oa_ref), (b_ref, ob_ref), (c_ref, oc_ref))
    copies = [pltpu.make_async_copy(i, o, sems.at[n]) for n, (i, o) in enumerate(pairs)]
    for copy in copies:
        copy.start()
    for copy in copies:
        copy.wait()


def store(results):
    shape = jax.ShapeDtypeStruct(results[0].shape, BF16)
    return pl.pallas_call(
        store_kernel,
        out_shape=(shape,) * 3,
        in_specs=[pl.BlockSpec(memory_space=pltpu.VMEM)] * 3,
        out_specs=(pl.BlockSpec(memory_space=pltpu.HBM),) * 3,
        scratch_shapes=[pltpu.SemaphoreType.DMA((3,))],
        compiler_params=pltpu.CompilerParams(vmem_limit_bytes=8 << 20),
    )(*results)


def build(mesh, Z, Y, X):
    def local(queries, key_heads, value_heads, grad_output, doc_lengths):
        tokens, heads, width = queries.shape
        all_tokens = tokens * Z * Y * X * 2
        scaling = 1.0 / math.sqrt(width * (all_tokens // 2))
        dims = (Z, Y, X, heads // 2, tokens)
        return store(exchange(dims, scaling, doc_lengths, queries, key_heads, value_heads, grad_output))

    placed = P(("seq", "head"), None, None)
    return jax.shard_map(
        local,
        mesh=mesh,
        in_specs=(placed,) * 4 + (P(),),
        out_specs=(placed,) * 3,
        check_vma=False,
    )


def solution(mesh):
    return build(mesh, mesh.shape["seq"] // 4, 4, mesh.shape["head"] // 2)
```

```python
import functools
import math

import jax
import jax.numpy as jnp
from jax import lax
from jax.experimental import pallas as pl
from jax.experimental.pallas import tpu as pltpu
from jax.sharding import PartitionSpec as P

MESH = pl.DeviceIdType.MESH
F32 = jnp.float32
BF16 = jnp.bfloat16
NDOC = 16
HD = 128


STEPS = (
    (0, 0), (2, 2), (0, 2), (2, 1), (0, 3), (1, 2), (3, 2), (2, 3),
    (3, 3), (1, 3), (3, 1), (2, 0), (1, 1), (3, 0), (0, 1), (1, 0),
)
STEPS_X = sum(dx << (2 * i) for i, (dx, dy) in enumerate(STEPS))
STEPS_Y = sum(dy << (2 * i) for i, (dx, dy) in enumerate(STEPS))


def dot(a, b, ca, cb):
    return lax.dot_general(a, b, (((ca,), (cb,)), ((), ())), preferred_element_type=F32)


def kernel(
    dims, scaling,
    len_hbm, q_ref, k_ref, v_ref, g_ref,
    oq_ref, ok_ref, ov_ref,
    raw, toks, sums, arrived, totals, zgot, ready, entering, part, outs, swapped, mask_f, mask_b,
    len_ref, ends, tab_p, tab_z,
    len_sem, own_sem, xs_sem, xr_sem, is_sem, ir_sem, zs_sem, zr_sem, os_sem, or_sem, last_sem, ys_sem, yr_sem, yl_sem,
):
    Z, Y, X, NH, TK = dims
    XY = X * Y
    CHUNKS = NH // XY
    PARTS = 2 * CHUNKS
    HALF = HD // 2
    CT = 2 * TK
    PT = XY * CT
    s = lax.axis_index("seq")
    hh = lax.axis_index("head")
    z, y = s // Y, s % Y
    x, c = hh // 2, hh % 2
    other = 1 - c
    me = y * X + x
    ins = (q_ref, k_ref, v_ref, g_ref)
    out_refs = (oq_ref, ok_ref, ov_ref)
    partner = (s, x * 2 + other)

    def at_plane(p):
        return (z * Y + p // X, (p % X) * 2 + c)

    def at_z(t):
        return (t * Y + y, hh)

    def plane_step(dx, dy):
        return (z * Y + (y + dy) % Y, ((x + dx) % X) * 2 + c)

    def offset(i):
        return (STEPS_X >> (2 * i)) & 3, (STEPS_Y >> (2 * i)) & 3

    def ahead(i):
        dx, dy = offset(i)
        return ((y + dy) % Y) * X + (x + dx) % X

    def behind(i):
        dx, dy = offset(i)
        return ((y - dy + Y) % Y) * X + (x - dx + X) % X

    def z_step(n):
        return (z + (((n + 1) // 2) if n % 2 else Z - n // 2)) % Z

    lengths = pltpu.make_async_copy(len_hbm, len_ref, len_sem)
    lengths.start()
    barrier = pltpu.get_barrier_semaphore()

    def greet(device):
        pl.semaphore_signal(barrier, inc=1, device_id=device, device_id_type=MESH)

    for n in range(Z - 1, 3, -1):
        greet(at_z(z_step(n)))
    for dx, dy in STEPS[1:]:
        greet(plane_step(dx, dy))
    for n in range(3, 0, -1):
        greet(at_z(z_step(n)))
    greet(partner)

    def own_copy(j, a):
        return pltpu.make_async_copy(
            ins[a].at[:, pl.ds(pl.multiple_of(c * NH + j * XY, 8), XY)],
            raw.at[a, j, c],
            own_sem.at[j, a],
        )

    def core_copy(j, a):
        return pltpu.make_async_remote_copy(
            src_ref=ins[a].at[:, pl.ds(pl.multiple_of(other * NH + j * XY, 8), XY)],
            dst_ref=raw.at[a, j, c],
            send_sem=xs_sem.at[j, a],
            recv_sem=xr_sem.at[j, a],
            device_id=partner,
            device_id_type=MESH,
        )

    def core_arrival(j, a):
        return pltpu.make_async_remote_copy(
            src_ref=ins[a].at[:, pl.ds(pl.multiple_of(other * NH + j * XY, 8), XY)],
            dst_ref=raw.at[a, j, other],
            send_sem=xs_sem.at[j, a],
            recv_sem=xr_sem.at[j, a],
            device_id=partner,
            device_id_type=MESH,
        )

    for j in range(CHUNKS):
        for a in range(4):
            own_copy(j, a).start()

    lengths.wait()
    total_len = jnp.int32(0)
    for d in range(NDOC):
        total_len = total_len + len_ref[d]
        ends[d] = total_len

    def same(low, high):
        cut = jnp.int32(0)
        for d in range(NDOC):
            e = ends[d]
            cut = cut + jnp.where((low < e) & (e <= high), 1, 0)
        return jnp.where(cut == 0, 1.0, 0.0).astype(F32)

    def fill_plane(p, carry):
        first = z * PT + p * CT
        last = first + CT - 1
        tab_p[0, p] = same(first - 1, last)
        tab_p[1, p] = same(first - 1, first)
        tab_p[2, p] = same(first, last + 1)
        tab_p[3, p] = same(last, last + 1)
        return carry

    def fill_z(t, carry):
        tab_z[0, t] = jnp.where(t < z, same((t + 1) * PT - 1, z * PT - 1), 0.0).astype(F32)
        tab_z[1, t] = jnp.where(t > z, same((z + 1) * PT, t * PT), 0.0).astype(F32)
        return carry

    base = (s * X + x) * CT
    rows = base + lax.broadcasted_iota(jnp.int32, (CT, CT), 0)
    cols = base + lax.broadcasted_iota(jnp.int32, (CT, CT), 1)
    row_doc = jnp.zeros((CT, CT), jnp.int32)
    col_doc = jnp.zeros((CT, CT), jnp.int32)
    first_doc = jnp.int32(0)
    last_doc = jnp.int32(0)
    for d in range(NDOC):
        e = ends[d]
        row_doc = row_doc + (e <= rows).astype(jnp.int32)
        col_doc = col_doc + (e <= cols).astype(jnp.int32)
        first_doc = first_doc + jnp.where(e <= base, 1, 0)
        last_doc = last_doc + jnp.where(e <= base + CT - 1, 1, 0)
    in_block = jnp.where((row_doc == col_doc) & (rows >= cols), scaling, 0.0).astype(F32)
    leading = jnp.where(row_doc == first_doc, 1.0, 0.0).astype(F32)
    trailing = jnp.where(row_doc == last_doc, 1.0, 0.0).astype(F32)
    mask_f[0] = in_block
    mask_f[1] = leading
    mask_f[2] = trailing
    mask_b[0] = leading.astype(BF16)
    mask_b[1] = trailing.astype(BF16)

    def tok(a, h):
        return toks[a, h].reshape(CT, HD)

    def swap_in(j, core):
        for a in range(4):
            toks[a, pl.ds(j * XY, XY), core] = jnp.swapaxes(raw[a, j, core], 0, 1)

    def send_sum(u, i):
        p = ahead(i)
        return pltpu.make_async_remote_copy(
            src_ref=sums.at[(u // 2) * XY + p, u % 2],
            dst_ref=arrived.at[u, me],
            send_sem=is_sem.at[u],
            recv_sem=ir_sem.at[u],
            device_id=at_plane(p),
            device_id_type=MESH,
        )

    def all_sums(u):
        block = arrived.at[u, pl.ds(0, XY - 1)]
        return pltpu.make_async_remote_copy(
            src_ref=block,
            dst_ref=block,
            send_sem=is_sem.at[u],
            recv_sem=ir_sem.at[u],
            device_id=partner,
            device_id_type=MESH,
        )

    def make_sums(j):
        def step(n, carry):
            i = n % XY
            h = j * XY + ahead(i)
            keys = tok(1, h) * mask_b[1]
            a_sum = (dot(tok(2, h), keys, 0, 0) * scaling).astype(BF16).reshape(2, HALF, HD)
            queries = tok(0, h) * mask_b[0]
            b_sum = (dot(tok(3, h), queries, 0, 0) * scaling).astype(BF16).reshape(2, HALF, HD)
            for r in range(2):
                sums[h, r, 0] = a_sum[r]
                sums[h, r, 1] = b_sum[r]

            @pl.when(i == 0)
            def _():
                for r in range(2):
                    arrived[2 * j + r, me, 0] = a_sum[r]
                    arrived[2 * j + r, me, 1] = b_sum[r]

            @pl.when(n >= 2)
            def _():
                send_sum(2 * j, n - 1).start()

            return carry

        lax.fori_loop(1, XY + 1, step, 0, unroll=2)

        for i in range(1, XY):
            send_sum(2 * j + 1, i).start()

    def local_work(low, high):
        def step(h, carry):
            q, k, v, g = (tok(a, h) for a in range(4))
            gs = (dot(g, v, 1, 1) * mask_f[0]).astype(BF16)
            sc = (dot(q, k, 1, 1) * mask_f[0]).astype(BF16)
            part[0, h] = dot(gs, k, 1, 0)
            part[1, h] = dot(gs, q, 0, 0)
            part[2, h] = dot(sc, g, 0, 0)
            return carry

        lax.fori_loop(low, high, step, 0)

    def z_copy(u, n):
        t = z_step(n)
        return pltpu.make_async_remote_copy(
            src_ref=totals.at[u, jnp.where(t < z, 1, 0)],
            dst_ref=zgot.at[u, z],
            send_sem=zs_sem.at[u],
            recv_sem=zr_sem.at[u],
            device_id=at_z(t),
            device_id_type=MESH,
        )

    def all_z(u):
        block = zgot.at[u, pl.ds(0, Z - 1)]
        return pltpu.make_async_remote_copy(
            src_ref=block,
            dst_ref=block,
            send_sem=zs_sem.at[u],
            recv_sem=zr_sem.at[u],
            device_id=partner,
            device_id_type=MESH,
        )

    def plane_totals(j):
        all_sums(j).wait_recv()

        def step(p, carry):
            a, b = carry
            r = XY - 1 - p
            a = tab_p[0, p] * a + arrived[j, p, 0].astype(F32)
            b = tab_p[2, r] * b + arrived[j, r, 1].astype(F32)
            return a, b

        zero = jnp.zeros((HALF, HD), F32)
        a, b = lax.fori_loop(0, XY, step, (zero, zero), unroll=4)
        totals[j, 0] = a
        totals[j, 1] = b

    def send_totals(j):
        for n in range(1, Z):
            z_copy(j, n).start()

    def entering_sem(u, p):
        return last_sem.at[p] if u == PARTS - 1 else or_sem.at[u]

    def send_entering(u, i):
        p = ahead(i)
        return pltpu.make_async_remote_copy(
            src_ref=ready.at[u, p],
            dst_ref=entering.at[(u // 2) * XY + me, u % 2],
            send_sem=os_sem.at[u],
            recv_sem=entering_sem(u, me),
            device_id=at_plane(p),
            device_id_type=MESH,
        )

    def last_entering(p):
        u = PARTS - 1
        return pltpu.make_async_remote_copy(
            src_ref=ready.at[u, p],
            dst_ref=entering.at[(u // 2) * XY + p, u % 2],
            send_sem=os_sem.at[u],
            recv_sem=entering_sem(u, p),
            device_id=at_plane(p),
            device_id_type=MESH,
        )

    def all_entering(u):
        block = ready.at[u, pl.ds(0, XY - 1)]
        return pltpu.make_async_remote_copy(
            src_ref=block,
            dst_ref=block,
            send_sem=os_sem.at[u],
            recv_sem=or_sem.at[min(u, PARTS - 2)],
            device_id=partner,
            device_id_type=MESH,
        )

    def make_entering(j):
        all_z(j).wait_recv()
        start = (jnp.zeros((HALF, HD), F32), jnp.zeros((HALF, HD), F32))
        for n in range(1, Z):
            t = z_step(n)
            got = zgot[j, t]
            start = (start[0] + tab_z[0, t] * got, start[1] + tab_z[1, t] * got)

        def step(p, carry):
            a, b = carry
            r = XY - 1 - p
            ready[j, p, 0] = (tab_p[1, p] * a).astype(BF16)
            ready[j, r, 1] = (tab_p[3, r] * b).astype(BF16)
            a = tab_p[0, p] * a + arrived[j, p, 0].astype(F32)
            b = tab_p[2, r] * b + arrived[j, r, 1].astype(F32)
            return a, b

        lax.fori_loop(0, XY, step, start, unroll=4)
        entering[(j // 2) * XY + me, j % 2] = ready[j, me]

        for i in range(1, XY):
            send_entering(j, i).start()

    def finish(j):
        last = j == CHUNKS - 1
        all_entering(2 * j).wait_recv()
        if not last:
            all_entering(2 * j + 1).wait_recv()

        def step(i, carry):
            p = behind(i)
            h = j * XY + p

            if last:

                @pl.when(i > 0)
                def _():
                    last_entering(p).wait_recv()

            a = entering[h, :, 0].reshape(HD, HD)
            b = entering[h, :, 1].reshape(HD, HD)
            dq = part[0, h] + mask_f[1] * dot(tok(3, h), a, 1, 0)
            dk = part[1, h] + mask_f[2] * dot(tok(2, h), b, 1, 0)
            dv = part[2, h] + mask_f[2] * dot(tok(1, h), b, 1, 1)
            outs[0, h] = dq.astype(BF16).reshape(2, TK, HD)
            outs[1, h] = dk.astype(BF16).reshape(2, TK, HD)
            outs[2, h] = dv.astype(BF16).reshape(2, TK, HD)
            return carry

        lax.fori_loop(0, XY, step, 0, unroll=2)

    def swap_out(j, a, core):
        swapped[a, j, core] = jnp.swapaxes(outs[a, pl.ds(j * XY, XY), core], 0, 1)

    def out_own(j, a):
        return pltpu.make_async_copy(
            swapped.at[a, j, c],
            out_refs[a].at[:, pl.ds(pl.multiple_of(c * NH + j * XY, 8), XY)],
            yl_sem.at[j, a],
        )

    def out_core(j, a):
        return pltpu.make_async_remote_copy(
            src_ref=swapped.at[a, j, other],
            dst_ref=out_refs[a].at[:, pl.ds(pl.multiple_of(c * NH + j * XY, 8), XY)],
            send_sem=ys_sem.at[j, a],
            recv_sem=yr_sem.at[j, a],
            device_id=partner,
            device_id_type=MESH,
        )

    def out_arrival(j, a):
        return pltpu.make_async_remote_copy(
            src_ref=swapped.at[a, j, other],
            dst_ref=out_refs[a].at[:, pl.ds(pl.multiple_of(other * NH + j * XY, 8), XY)],
            send_sem=ys_sem.at[j, a],
            recv_sem=yr_sem.at[j, a],
            device_id=partner,
            device_id_type=MESH,
        )

    for j in range(CHUNKS):
        for a in range(4):
            own_copy(j, a).wait()
        swap_in(j, c)
    pl.semaphore_wait(barrier, XY + Z - 1)
    for j in range(CHUNKS):
        for a in range(4):
            core_copy(j, a).start()
    for j in range(CHUNKS):
        for a in range(4):
            core_arrival(j, a).wait_recv()
        swap_in(j, other)
        make_sums(j)
    lax.fori_loop(0, XY, fill_plane, 0)
    lax.fori_loop(0, Z, fill_z, 0)

    def gather(u):
        plane_totals(u)
        send_totals(u)

    piece = NH // PARTS
    for u in range(PARTS):
        local_work(u * piece, (u + 1) * piece)
        if u == PARTS - 1:
            make_entering(u - 2)
        gather(u)
        if 2 <= u < PARTS - 1:
            make_entering(u - 2)
    make_entering(PARTS - 2)
    make_entering(PARTS - 1)
    for j in range(CHUNKS):
        for a in range(4):
            core_copy(j, a).wait_send()
    for u in range(PARTS):
        all_sums(u).wait_send()
        all_z(u).wait_send()
    for j in range(CHUNKS):
        finish(j)
        for a in range(3):
            swap_out(j, a, other)
            out_core(j, a).start()
        for a in range(3):
            swap_out(j, a, c)
            out_own(j, a).start()

    for u in range(PARTS):
        all_entering(u).wait_send()
    for j in range(CHUNKS):
        for a in range(3):
            out_own(j, a).wait()
            out_core(j, a).wait_send()
            out_arrival(j, a).wait_recv()


def exchange(dims, scaling, lengths, q, k, v, g):
    Z, Y, X, NH, TK = dims
    XY = X * Y
    CHUNKS = NH // XY
    CT = 2 * TK
    PARTS = 2 * CHUNKS
    HALF = HD // 2
    shape = jax.ShapeDtypeStruct((TK, 2 * NH, HD), BF16)
    dma = pltpu.SemaphoreType.DMA
    return pl.pallas_call(
        functools.partial(kernel, dims, scaling),
        out_shape=(shape, shape, shape),
        in_specs=[pl.BlockSpec(memory_space=pl.ANY)] * 5,
        out_specs=(pl.BlockSpec(memory_space=pl.ANY),) * 3,
        scratch_shapes=[
            pltpu.VMEM((4, CHUNKS, 2, TK, XY, HD), BF16),
            pltpu.VMEM((4, NH, 2, TK, HD), BF16),
            pltpu.VMEM((NH, 2, 2, HALF, HD), BF16),
            pltpu.VMEM((PARTS, XY, 2, HALF, HD), BF16),
            pltpu.VMEM((PARTS, 2, HALF, HD), F32),
            pltpu.VMEM((PARTS, Z, HALF, HD), F32),
            pltpu.VMEM((PARTS, XY, 2, HALF, HD), BF16),
            pltpu.VMEM((NH, 2, 2, HALF, HD), BF16),
            pltpu.VMEM((3, NH, CT, HD), F32),
            pltpu.VMEM((3, NH, 2, TK, HD), BF16),
            pltpu.VMEM((3, CHUNKS, 2, TK, XY, HD), BF16),
            pltpu.VMEM((3, CT, HD), F32),
            pltpu.VMEM((2, CT, HD), BF16),
            pltpu.SMEM((NDOC,), jnp.int32),
            pltpu.SMEM((NDOC,), jnp.int32),
            pltpu.SMEM((4, XY), F32),
            pltpu.SMEM((2, Z), F32),
            dma,
            dma((CHUNKS, 4)),
            dma((CHUNKS, 4)),
            dma((CHUNKS, 4)),
            dma((PARTS,)),
            dma((PARTS,)),
            dma((PARTS,)),
            dma((PARTS,)),
            dma((PARTS,)),
            dma((PARTS - 1,)),
            dma((XY,)),
            dma((CHUNKS, 3)),
            dma((CHUNKS, 3)),
            dma((CHUNKS, 3)),
        ],
        compiler_params=pltpu.CompilerParams(
            collective_id=0, has_side_effects=True, vmem_limit_bytes=50 << 20
        ),
    )(lengths, q, k, v, g)


def store_kernel(a_ref, b_ref, c_ref, oa_ref, ob_ref, oc_ref, sems):
    pairs = ((a_ref, oa_ref), (b_ref, ob_ref), (c_ref, oc_ref))
    copies = [pltpu.make_async_copy(i, o, sems.at[n]) for n, (i, o) in enumerate(pairs)]
    for copy in copies:
        copy.start()
    for copy in copies:
        copy.wait()


def store(results):
    shape = jax.ShapeDtypeStruct(results[0].shape, BF16)
    return pl.pallas_call(
        store_kernel,
        out_shape=(shape,) * 3,
        in_specs=[pl.BlockSpec(memory_space=pltpu.VMEM)] * 3,
        out_specs=(pl.BlockSpec(memory_space=pltpu.HBM),) * 3,
        scratch_shapes=[pltpu.SemaphoreType.DMA((3,))],
        compiler_params=pltpu.CompilerParams(vmem_limit_bytes=8 << 20),
    )(*results)


def build(mesh, Z, Y, X):
    def local(queries, key_heads, value_heads, grad_output, doc_lengths):
        tokens, heads, width = queries.shape
        all_tokens = tokens * Z * Y * X * 2
        scaling = 1.0 / math.sqrt(width * (all_tokens // 2))
        dims = (Z, Y, X, heads // 2, tokens)
        return store(exchange(dims, scaling, doc_lengths, queries, key_heads, value_heads, grad_output))

    placed = P(("seq", "head"), None, None)
    return jax.shard_map(
        local,
        mesh=mesh,
        in_specs=(placed,) * 4 + (P(),),
        out_specs=(placed,) * 3,
        check_vma=False,
    )


def solution(mesh):
    return build(mesh, mesh.shape["seq"] // 4, 4, mesh.shape["head"] // 2)
```
